128 devices in a mesh: wide: 32 (over y, x, core), narrow: 4 (over z).
Axes of the slice: x: 4, y: 4, z: 4, core: 2. Of those that a mesh axis runs over, the one named last changes fastest.
Arguments:
- amplitudes: bfloat16 [48, 2, 1536, 1536], P('narrow', None, 'wide'), may hold values from -6 to 6
- pair_integrals: bfloat16 [48, 2, 1536, 1536], P('narrow', None, 'wide'), may hold values from -4 to 4
- cycle_integrals: bfloat16 [2, 1536, 2, 1536], P(None, None, None, 'narrow'), may hold values from -0.109375 to 0.109375
- ladder_integrals: bfloat16 [4, 4, 1536, 1536], P(None, None, 'wide', 'narrow'), may hold values from -0.078125 to 0.078125
- occ_energy: float32 [300], replicated, may hold values from -2 to -0.5
- virt_energy: float32 [1536], replicated, may hold values from 0.3 to 3
- occ_irrep: int32 [300], replicated, may hold values from 0 to 1
- virt_irrep: int32 [96], replicated, may hold values from 0 to 1
- slab_i: int32 [48], P('narrow'), may hold values from 0 to 299
- slab_j: int32 [2], replicated, may hold values from 0 to 299
Outputs:
- new_amplitudes: bfloat16 [48, 2, 1536, 1536], P('narrow', None, 'wide')
The draws below stay inside these ranges and needn't reach their ends.
Inputs may be any that keep to these rules, and one draw needn't show every extreme that they name: `slab_i`: each entry names an occupied orbital. `slab_j`: each entry names an occupied orbital.
All inputs are finite; a program needn't handle non-finite values.
Results may differ from the reference program's by a relative error of at most 0.0046.
Values may be sent and summed in bfloat16 or wider, within the bound.
A program may use at most 192 MiB of HBM per device.

```python
import jax
import jax.numpy as jnp
from jax import lax

NV = 1536
NOCC = 300
NJ = 2
NI = 48
TILE = 4
VBLK = 16


def plant(values, rng, least, top_value):
    index_at = [jax.random.randint(jax.random.fold_in(rng, axis), (), 0, length) for axis, length in enumerate(values.shape)]
    longest = values.shape.index(max(values.shape))
    neighbour = index_at[:longest] + [(index_at[longest] + 1) % values.shape[longest]] + index_at[longest + 1:]
    return values.at[tuple(index_at)].set(least).at[tuple(neighbour)].set(top_value)


def levels(key, dims, split, smallest, top_value):
    loudness = 1.0
    for axis_at, blocks in split:
        heights = jax.random.uniform(jax.random.fold_in(jax.random.fold_in(key, 6), axis_at), (blocks,), jnp.float32, smallest / len(split), top_value / len(split))
        loudness = loudness * jnp.repeat(jnp.exp(heights), dims[axis_at] // blocks).reshape((-1,) + (1,) * (len(dims) - 1 - axis_at))
    return loudness


def noise(key, dims, deviation, most, pieces=(), kind=jnp.bfloat16):
    values = jax.random.normal(key, dims, jnp.float32) * deviation
    if len(pieces) > 0:
        values = levels(key, dims, pieces, -0.22, 0.18) * values
    return jnp.clip(values, min=-most, max=most).astype(kind)


def setup_inputs(seed: int = 0) -> dict:
    keys = jax.random.split(jax.random.key(seed), 11)
    return {
        "amplitudes": noise(keys[0], (NI, NJ, NV, NV), 1.0, 6.0, ((0, 4), (2, 32))),
        "pair_integrals": noise(keys[1], (NI, NJ, NV, NV), 0.5, 4.0, ((0, 4), (2, 32))),
        "cycle_integrals": noise(keys[2], (NJ, NV, NJ, NV), (NJ * NV) ** -0.5, 0.109375, ((3, 4),)),
        "ladder_integrals": noise(keys[3], (TILE, TILE, NV, NV), (TILE * NV) ** -0.5, 0.078125, ((2, 32), (3, 4))),
        "occ_energy": jnp.clip(jax.random.uniform(keys[4], (NOCC,), jnp.float32, -2.0, -0.5), -2.0, -0.5),
        "virt_energy": jnp.clip(jax.random.uniform(keys[5], (NV,), jnp.float32, 0.3, 3.0), 0.3, 3.0),
        "occ_irrep": plant(jax.random.randint(keys[6], (NOCC,), 0, 2), jax.random.fold_in(keys[6], 1), 0, 1).astype(jnp.int32),
        "virt_irrep": plant(jax.random.randint(keys[7], (NV // VBLK,), 0, 2), jax.random.fold_in(keys[7], 1), 0, 1).astype(jnp.int32),
        "slab_i": plant(jax.random.randint(keys[8], (NI,), 0, NOCC), jax.random.fold_in(keys[8], 1), 0, NOCC - 1).astype(jnp.int32),
        "slab_j": jax.random.randint(keys[9], (NJ,), 0, NOCC).astype(jnp.int32),
    }


def reference(amplitudes, pair_integrals, cycle_integrals, ladder_integrals, occ_energy, virt_energy, occ_irrep, virt_irrep, slab_i, slab_j):
    cycle_full = cycle_integrals.astype(jnp.float32)

    def cycle_slice(amp_row):
        return jnp.einsum("kcb,kcja->jab", amp_row.astype(jnp.float32), cycle_full).astype(jnp.bfloat16)

    cycle = lax.map(cycle_slice, amplitudes)
    tile_amps = amplitudes[:, :, :TILE, :].astype(jnp.float32)
    ladder = jnp.einsum("ijcd,acbd->ijab", tile_amps, ladder_integrals.astype(jnp.float32))
    coupled = cycle.astype(jnp.float32).at[:, :, :TILE, :].add(ladder).astype(jnp.bfloat16)
    energy_first = occ_energy[slab_i]
    energy_second = occ_energy[slab_j]
    label_first = occ_irrep[slab_i]
    label_second = occ_irrep[slab_j]
    label_virt = jnp.repeat(virt_irrep, VBLK)
    residual = pair_integrals.astype(jnp.float32) + coupled.astype(jnp.float32)
    denominator = (virt_energy[None, None, :, None] + virt_energy[None, None, None, :]
                   - energy_first[:, None, None, None] - energy_second[None, :, None, None])
    parity = (label_first[:, None, None, None] + label_second[None, :, None, None]
              + label_virt[None, None, :, None] + label_virt[None, None, None, :]) % 2
    allowed = (1 - parity).astype(jnp.float32)
    return (allowed * residual / denominator).astype(jnp.bfloat16)
```

```python
import jax
import jax.numpy as jnp
from jax import lax
from jax.experimental import pallas as pl
from jax.experimental.pallas import tpu as pltpu
from jax.sharding import PartitionSpec as P

MESH = pl.DeviceIdType.MESH
BF16 = jnp.bfloat16
F32 = jnp.float32
VBLK = 16
SIDE = 4
CHIPS = SIDE * SIDE
PLANE = 2 * CHIPS
CHUNKS = 3
GROUP = 16


def remote(src, dst, send_sem, recv_sem, device):
    return pltpu.make_async_remote_copy(
        src_ref=src, dst_ref=dst, send_sem=send_sem, recv_sem=recv_sem, device_id=device, device_id_type=MESH
    )


def await_bytes(ref, sem):
    pltpu.make_async_copy(ref, ref, sem).wait()


def exchange_kernel(
    amp, wraw, vint, coupled, lad_out,
    wraw_v, v_v, head_v, wt, a_all, prod, tile_out, tile_in, part, part_in, sum_v, fin_in, lad_v,
    load_sem, s1, r1, sf, rf, wsend, wrecv, wfsend, wfrecv, csend, crecv,
    tz_send, tz_recv, tb_send, tb_recv, tf_send, p_send, p_recv, f_send, f_recv,
):
    p = lax.axis_index("wide")
    z = lax.axis_index("narrow")
    core = lax.rem(p, 2)
    chip = lax.div(p, 2)
    x = lax.rem(chip, SIDE)
    y = lax.div(chip, SIDE)
    partner = (p + 1 - 2 * core, z)
    up = (p, lax.rem(z + 1, SIDE))
    down = (p, lax.rem(z + SIDE - 1, SIDE))
    z_up = lax.rem(z + 1, SIDE)
    z_down = lax.rem(z + SIDE - 1, SIDE)
    z_far = lax.rem(z + 2, SIDE)
    n_i, n_k, rows, n_b = amp.shape
    per_i = n_i // SIDE
    per_b = n_b // SIDE
    n_c = rows * PLANE
    depth = n_k * n_c

    load_w = pltpu.make_async_copy(wraw, wraw_v, load_sem.at[0])
    load_v = pltpu.make_async_copy(vint, v_v, load_sem.at[1])
    load_h = pltpu.make_async_copy(amp.at[:, :, pl.ds(0, 16), :], head_v, load_sem.at[2])
    load_w.start()
    load_v.start()

    @pl.when(p == 0)
    def _():
        load_h.start()

    barrier = pltpu.get_barrier_semaphore()

    def greet(step, carry):
        pl.semaphore_signal(barrier, inc=1, device_id=(lax.rem(p + step, PLANE), z), device_id_type=MESH)
        return carry

    lax.fori_loop(1, PLANE, greet, 0)

    def greet_z(step, carry):
        pl.semaphore_signal(barrier, inc=1, device_id=(p, lax.rem(z + step, SIDE)), device_id_type=MESH)
        return carry

    lax.fori_loop(1, SIDE, greet_z, 0)
    pl.semaphore_wait(barrier, PLANE - 1 + SIDE - 1)

    def a_rows(source_chip, source_core):
        return pl.ds(pl.multiple_of((2 * source_chip + source_core) * rows, rows), rows)

    def a_piece(dest_chip, i):
        dest_x = lax.rem(dest_chip, SIDE)
        dest_y = lax.div(dest_chip, SIDE)
        src = amp.at[dest_y * per_i + i, :, :, pl.ds(pl.multiple_of(dest_x * per_b, per_b), per_b)]
        dst = a_all.at[:, a_rows(chip, core), pl.ds(i * per_b, per_b)]
        return src, dst

    for i in range(per_i):
        src, dst = a_piece(chip, i)
        pltpu.make_async_copy(src, dst, r1.at[chip]).start()

    def send_a(step, carry):
        dest = lax.rem(chip + step, CHIPS)
        for i in range(per_i):
            src, dst = a_piece(dest, i)
            remote(src, dst, s1.at[dest], r1.at[chip], (2 * dest + core, z)).start()
        return carry

    lax.fori_loop(1, CHIPS, send_a, 0)

    @pl.when(p == 0)
    def _():
        load_h.wait()
        pairs = n_i * n_k
        flat = head_v[...].reshape(pairs * 16, n_b)
        r = lax.broadcasted_iota(jnp.int32, (pairs, pairs * 16), 0)
        c = lax.broadcasted_iota(jnp.int32, (pairs, pairs * 16), 1)
        for t in range(4):
            pick = jnp.where(c == 16 * r + t, 1.0, 0.0).astype(BF16)
            one = jnp.dot(pick, flat, preferred_element_type=F32).astype(BF16)
            for zz in range(SIDE):
                tile_out[zz, t] = one[:, zz * per_b : (zz + 1) * per_b]
        pltpu.make_async_copy(tile_out.at[z], tile_in.at[z], tz_recv.at[z]).start()

        def send_t(step, carry):
            zz = lax.rem(z + step, SIDE)
            remote(tile_out.at[zz], tile_in.at[z], tz_send.at[zz], tz_recv.at[z], (p, zz)).start()
            return carry

        lax.fori_loop(1, SIDE, send_t, 0)

    load_w.wait()
    r = lax.broadcasted_iota(jnp.int32, (256, 128), 0)
    c = lax.broadcasted_iota(jnp.int32, (256, 128), 1)
    pick = jnp.where(r == 2 * c + core, 1.0, 0.0).astype(BF16)
    for k in range(n_k):

        def prep(block, carry):
            at = pl.multiple_of(block * 128, 128)
            both = wraw_v[k, pl.ds(at, 128), :, :].reshape(256, per_b)
            turned = lax.dot_general(both, pick, (((0,), (0,)), ((), ())), preferred_element_type=F32)
            turned = turned.astype(BF16)
            for g in range(per_b // GROUP):
                wt[z, g % CHUNKS, g // CHUNKS, :, pl.ds(pl.multiple_of(k * n_c + at, 128), 128)] = turned[
                    g * GROUP : (g + 1) * GROUP
                ]
            return carry

        lax.fori_loop(0, n_c // 128, prep, 0)

    def w_own(t, way):
        return remote(wt.at[z, t], wt.at[z, t], wsend.at[way, t], wrecv.at[way, t], (up, down)[way])

    half = pl.ds(0, 4), pl.ds(4, 4)

    def w_pass(t, way):
        source = (z_down, z_up)[way]
        ref = wt.at[source, t, half[way]]
        return remote(ref, ref, wfsend.at[way, t], wfrecv.at[way, t], (up, down)[way])

    def w_got(t, way):
        await_bytes(wt.at[(z_down, z_up)[way], t], wrecv.at[way, t])

    def w_far(t, way):
        await_bytes(wt.at[z_far, t, half[way]], wfrecv.at[way, t])

    for way in range(2):
        w_own(0, way).start()
    for way in range(2):
        w_own(1, way).start()

    def pass_a(step, carry):
        source = lax.rem(chip + CHIPS - step, CHIPS)
        ref = a_all.at[:, a_rows(source, core), :]
        await_bytes(ref, r1.at[source])
        remote(ref, ref, sf.at[source], rf.at[source], partner).start()
        return carry

    lax.fori_loop(0, 4, pass_a, 0)

    @pl.when(p == 0)
    def _():
        for zz in range(SIDE):
            await_bytes(tile_in.at[zz], tz_recv.at[zz])

        def send_b(step, carry):
            remote(tile_in, tile_in, tb_send.at[step], tb_recv, (2 * step, z)).start()
            return carry

        lax.fori_loop(1, CHIPS, send_b, 0)

    lax.fori_loop(4, 8, pass_a, 0)

    @pl.when(p != 0)
    def _():
        await_bytes(tile_in, tb_recv)

    @pl.when(core == 0)
    def _():
        remote(tile_in, tile_in, tf_send, tb_recv, partner).start()

    load_v.wait()
    for zz in range(SIDE):
        total = None
        for t in range(4):
            right = v_v[:, t].reshape(4 * rows, per_b)
            term = lax.dot_general(
                tile_in[zz, t], right, (((1,), (1,)), ((), ())), preferred_element_type=F32
            )
            total = term if total is None else total + term
        part[zz] = total
    pltpu.make_async_copy(part.at[z], part_in.at[z], p_recv.at[z]).start()

    def send_p(step, carry):
        zz = lax.rem(z + step, SIDE)
        remote(part.at[zz], part_in.at[z], p_send.at[zz], p_recv.at[z], (p, zz)).start()
        return carry

    lax.fori_loop(1, SIDE, send_p, 0)

    for way in range(2):
        w_got(0, way)
        w_pass(0, way).start()
        w_own(2, way).start()

    lax.fori_loop(8, 12, pass_a, 0)

    for zz in range(SIDE):
        await_bytes(part_in.at[zz], p_recv.at[zz])
    sum_v[...] = part_in[0] + part_in[1] + part_in[2] + part_in[3]

    @pl.when(p == 0)
    def _():
        pltpu.make_async_copy(sum_v, fin_in.at[0], f_recv).start()

    @pl.when(p != 0)
    def _():
        remote(sum_v, fin_in.at[p], f_send, f_recv, (0, z)).start()

    lax.fori_loop(12, CHIPS, pass_a, 0)

    for way in range(2):
        w_got(1, way)
        w_pass(1, way).start()

    def got_a(step, carry):
        source = lax.rem(chip + CHIPS - step, CHIPS)
        await_bytes(a_all.at[:, a_rows(source, 1 - core), :], rf.at[source])
        return carry

    lax.fori_loop(0, CHIPS, got_a, 0)

    def target(t):
        return coupled.at[
            pl.ds(y * per_i, per_i), core, pl.ds(t * GROUP, GROUP), pl.ds(pl.multiple_of(x * per_b, per_b), per_b)
        ]

    def product(t):
        left = wt[:, t].reshape(PLANE * GROUP, depth)
        for start, size in ((0, 512), (512, 512), (1024, 128)):
            right = a_all[:, :, start : start + size].reshape(depth, size)
            value = jnp.dot(left, right, preferred_element_type=F32).astype(BF16)
            for lane in range(0, size, 128):
                i, at = (start + lane) // per_b, (start + lane) % per_b
                prod[t, :, i, :, at : at + 128] = value[:, lane : lane + 128].reshape(PLANE, GROUP, 128)
        pltpu.make_async_copy(prod.at[t, p], target(t), crecv).start()

        def send_c(step, carry):
            q = lax.rem(p + step, PLANE)
            remote(prod.at[t, q], target(t), csend.at[t], crecv, (q, z)).start()
            return carry

        lax.fori_loop(1, PLANE, send_c, 0)

    for t in range(CHUNKS):
        if t == 2:
            for way in range(2):
                w_got(2, way)
                w_pass(2, way).start()
        for way in range(2):
            w_far(t, way)
        product(t)
        if t == 0:

            @pl.when(p == 0)
            def _():
                await_bytes(fin_in, f_recv)
                for q in range(PLANE):
                    for a in range(4):
                        lad_v[a, :, q * rows : (q + 1) * rows] = fin_in[q, :, a * rows : (a + 1) * rows]
                pltpu.make_async_copy(lad_v, lad_out, load_sem.at[2]).start()

    def sent_a(step, carry):
        other = lax.rem(chip + step, CHIPS)
        await_bytes(a_all.at[:, a_rows(other, core), :], s1.at[other])
        return carry

    lax.fori_loop(1, CHIPS, sent_a, 0)

    def passed_a(step, carry):
        await_bytes(a_all.at[:, a_rows(step, core), :], sf.at[step])
        return carry

    lax.fori_loop(0, CHIPS, passed_a, 0)
    for way in range(2):
        for t in range(CHUNKS):
            await_bytes(wt.at[z, t], wsend.at[way, t])
            await_bytes(wt.at[z, t, half[way]], wfsend.at[way, t])

    def sent_p(step, carry):
        zz = lax.rem(z + step, SIDE)
        await_bytes(part.at[zz], p_send.at[zz])
        return carry

    lax.fori_loop(1, SIDE, sent_p, 0)

    @pl.when(core == 0)
    def _():
        await_bytes(tile_in, tf_send)

    @pl.when(p == 0)
    def _():
        def sent_t(step, carry):
            zz = lax.rem(z + step, SIDE)
            await_bytes(tile_out.at[zz], tz_send.at[zz])
            return carry

        lax.fori_loop(1, SIDE, sent_t, 0)

        def sent_b(step, carry):
            await_bytes(tile_in, tb_send.at[step])
            return carry

        lax.fori_loop(1, CHIPS, sent_b, 0)
        await_bytes(lad_v, load_sem.at[2])

    @pl.when(p != 0)
    def _():
        await_bytes(sum_v, f_send)

    for t in range(CHUNKS):
        await_bytes(prod.at[t, pl.ds(0, PLANE - 1)], csend.at[t])
    await_bytes(coupled, crecv)


def exchange(amp, wraw, vint):
    n_i, n_k, rows, n_b = amp.shape
    per_i, per_b, n_c = n_i // SIDE, n_b // SIDE, rows * PLANE
    dma = pltpu.SemaphoreType.DMA
    anywhere = pl.BlockSpec(memory_space=pl.ANY)
    return pl.pallas_call(
        exchange_kernel,
        out_shape=(
            jax.ShapeDtypeStruct(amp.shape, BF16),
            jax.ShapeDtypeStruct((4, n_i * n_k, n_b), F32),
        ),
        in_specs=[anywhere] * 3,
        out_specs=(anywhere, anywhere),
        scratch_shapes=[
            pltpu.VMEM(wraw.shape, BF16),
            pltpu.VMEM(vint.shape, BF16),
            pltpu.VMEM((n_i, n_k, 16, n_b), BF16),
            pltpu.VMEM((SIDE, CHUNKS, 8, GROUP, n_k * n_c), BF16),
            pltpu.VMEM((n_k, n_c, per_i * per_b), BF16),
            pltpu.VMEM((CHUNKS, PLANE, per_i, GROUP, per_b), BF16),
            pltpu.VMEM((SIDE, 4, n_i * n_k, per_b), BF16),
            pltpu.VMEM((SIDE, 4, n_i * n_k, per_b), BF16),
            pltpu.VMEM((SIDE, n_i * n_k, 4 * rows), F32),
            pltpu.VMEM((SIDE, n_i * n_k, 4 * rows), F32),
            pltpu.VMEM((n_i * n_k, 4 * rows), F32),
            pltpu.VMEM((PLANE, n_i * n_k, 4 * rows), F32),
            pltpu.VMEM((4, n_i * n_k, n_b), F32),
            dma((3,)),
            dma((CHIPS,)),
            dma((CHIPS,)),
            dma((CHIPS,)),
            dma((CHIPS,)),
            dma((2, CHUNKS)),
            dma((2, CHUNKS)),
            dma((2, CHUNKS)),
            dma((2, CHUNKS)),
            dma((CHUNKS,)),
            dma,
            dma((SIDE,)),
            dma((SIDE,)),
            dma((CHIPS,)),
            dma,
            dma,
            dma((SIDE,)),
            dma((SIDE,)),
            dma,
            dma,
        ],
        compiler_params=pltpu.CompilerParams(
            collective_id=0, has_side_effects=True, vmem_limit_bytes=60 * 1024 * 1024
        ),
        name="exchange",
    )(amp, wraw, vint)


def update_kernel(
    coupled, pair, lad, occ_e, occ_l, slab_i, slab_j, virt_e, virt_l, out, sum_ab, odd_ab
):
    p = lax.axis_index("wide")
    step = pl.program_id(0)
    rows, n_b = sum_ab.shape

    @pl.when(step == 0)
    def _():
        row = lax.broadcasted_iota(jnp.int32, (rows, n_b), 0)
        col = lax.broadcasted_iota(jnp.int32, (rows, n_b), 1)
        mine = col == row + p * rows
        energy = jnp.broadcast_to(virt_e[...], (rows, n_b))
        sum_ab[...] = energy + jnp.sum(jnp.where(mine, energy, 0.0), axis=1, keepdims=True)
        blocks = virt_l.shape[1]
        block = lax.broadcasted_iota(jnp.int32, (blocks, n_b), 0)
        first = block * VBLK
        at = lax.broadcasted_iota(jnp.int32, (blocks, n_b), 1)
        member = jnp.where((at >= first) & (at < first + VBLK), 1.0, 0.0).astype(BF16)
        labels = jnp.broadcast_to((virt_l[...] & 1).astype(F32).astype(BF16), (8, blocks))
        label = jnp.dot(labels, member, preferred_element_type=F32)
        label = jnp.broadcast_to(label[0:1], (rows, n_b))
        label_row = jnp.sum(jnp.where(mine, label, 0.0), axis=1, keepdims=True)
        odd_ab[...] = jnp.abs(label - label_row)

    energy_i = occ_e[slab_i[step]]
    label_i = occ_l[slab_i[step]]
    for j in range(coupled.shape[1]):
        energy = energy_i + occ_e[slab_j[j]]
        odd = ((label_i + occ_l[slab_j[j]]) & 1).astype(F32)

        def update(value, count):
            residual = pair[0, j, 0:count].astype(F32) + value
            allowed = (1.0 - odd) + (2.0 * odd - 1.0) * odd_ab[0:count]
            return (allowed * residual / (sum_ab[0:count] - energy)).astype(BF16)

        out[0, j] = update(coupled[0, j].astype(F32), rows)

        @pl.when(p == 0)
        def _():
            at = step * coupled.shape[1] + j
            term = jnp.concatenate(
                [lad[a, pl.ds(at, 1), :] for a in range(4)] + [jnp.zeros((12, n_b), F32)], axis=0
            )
            value = (coupled[0, j, 0:16].astype(F32) + term).astype(BF16).astype(F32)
            out[0, j, 0:16] = update(value, 16)


def denominator_update(coupled, pair, lad, occ_e, virt_e, occ_l, virt_l, slab_i, slab_j):
    n_i, n_j, rows, n_b = pair.shape
    block = pl.BlockSpec((1, n_j, rows, n_b), lambda i: (i, 0, 0, 0))
    scalars = pl.BlockSpec(memory_space=pltpu.SMEM)
    return pl.pallas_call(
        update_kernel,
        grid=(n_i,),
        out_shape=jax.ShapeDtypeStruct(pair.shape, BF16),
        in_specs=[
            block,
            block,
            pl.BlockSpec(lad.shape, lambda i: (0, 0, 0)),
            scalars,
            scalars,
            scalars,
            scalars,
            pl.BlockSpec((1, n_b), lambda i: (0, 0)),
            pl.BlockSpec((1, virt_l.shape[0]), lambda i: (0, 0)),
        ],
        out_specs=block,
        scratch_shapes=[pltpu.VMEM((rows, n_b), F32), pltpu.VMEM((rows, n_b), F32)],
        name="update",
    )(coupled, pair, lad, occ_e, occ_l, slab_i, slab_j, virt_e.reshape(1, -1), virt_l.reshape(1, -1))


def per_device(
    amplitudes,
    pair_integrals,
    cycle_integrals,
    ladder_integrals,
    occ_energy,
    virt_energy,
    occ_irrep,
    virt_irrep,
    slab_i,
    slab_j,
):
    coupled, lad = exchange(amplitudes, cycle_integrals, ladder_integrals)
    return denominator_update(
        coupled, pair_integrals, lad, occ_energy, virt_energy, occ_irrep, virt_irrep, slab_i, slab_j
    )


def solution(mesh):
    return jax.shard_map(
        per_device,
        mesh=mesh,
        in_specs=(
            P("narrow", None, "wide", None),
            P("narrow", None, "wide", None),
            P(None, None, None, "narrow"),
            P(None, None, "wide", "narrow"),
            P(),
            P(),
            P(),
            P(),
            P("narrow"),
            P(),
        ),
        out_specs=P("narrow", None, "wide", None),
        check_vma=False,
    )
```

```python
import jax
import jax.numpy as jnp
from jax import lax
from jax.experimental import pallas as pl
from jax.experimental.pallas import tpu as pltpu
from jax.sharding import PartitionSpec as P

MESH = pl.DeviceIdType.MESH
BF16 = jnp.bfloat16
F32 = jnp.float32
VBLK = 16
SIDE = 4
CHIPS = SIDE * SIDE
PLANE = 2 * CHIPS
CHUNKS = 3
GROUP = 16
PARTS = 2 * CHUNKS
DIRECT = ((1, 0), (3, 0), (0, 1), (0, 3), (1, 1), (1, 3), (3, 1), (3, 3), (2, 0), (0, 2), (2, 2))
RELAYED = (((2, 1), (3, 0)), ((2, 3), (3, 0)), ((1, 2), (1, 3)), ((3, 2), (3, 3)))


def remote(src, dst, send_sem, recv_sem, device):
    return pltpu.make_async_remote_copy(
        src_ref=src, dst_ref=dst, send_sem=send_sem, recv_sem=recv_sem, device_id=device, device_id_type=MESH
    )


def await_bytes(ref, sem):
    pltpu.make_async_copy(ref, ref, sem).wait()


def exchange_kernel(
    amp, wraw, vint, virt_e, virt_l, coupled, lad_out, table_out,
    wraw_v, v_v, head_v, wt, a_all, prod, a_relay, c_relay, tile_out, tile_in, part, part_in, sum_v, fin_in, lad_v, table,
    load_sem, s1, r1, rs, rr, sf, rf, wsend, wrecv, wfsend, wfrecv, csend, crecv, crs, crr,
    tz_send, tz_recv, tb_send, tb_recv, tf_send, p_send, p_recv, f_send, f_recv,
):
    p = lax.axis_index("wide")
    z = lax.axis_index("narrow")
    core = lax.rem(p, 2)
    chip = lax.div(p, 2)
    x = lax.rem(chip, SIDE)
    y = lax.div(chip, SIDE)
    partner = (p + 1 - 2 * core, z)
    z_up = lax.rem(z + 1, SIDE)
    z_down = lax.rem(z + SIDE - 1, SIDE)
    z_far = lax.rem(z + 2, SIDE)
    neighbour = ((p, z_up), (p, z_down))
    z_source = (z_down, z_up)
    n_i, n_k, rows, n_b = amp.shape
    per_i = n_i // SIDE
    per_b = n_b // SIDE
    n_c = rows * PLANE
    depth = n_k * n_c
    pairs = n_i * n_k

    def place(offset):
        return lax.rem(x + offset[0] + SIDE, SIDE), lax.rem(y + offset[1] + SIDE, SIDE)

    def chip_at(offset):
        at_x, at_y = place(offset)
        return at_y * SIDE + at_x

    def back(offset):
        return (-offset[0], -offset[1])

    def beyond(dest, via):
        return ((dest[0] - via[0]) % SIDE, (dest[1] - via[1]) % SIDE)

    load_w = pltpu.make_async_copy(wraw, wraw_v, load_sem.at[0])
    load_v = pltpu.make_async_copy(vint, v_v, load_sem.at[1])
    load_h = pltpu.make_async_copy(amp.at[:, :, pl.ds(0, 16), :], head_v, load_sem.at[2])
    load_w.start()
    load_v.start()

    @pl.when(p == 0)
    def _():
        load_h.start()

    barrier = pltpu.get_barrier_semaphore()

    def greet(step, carry):
        pl.semaphore_signal(barrier, inc=1, device_id=(lax.rem(p + step, PLANE), z), device_id_type=MESH)
        return carry

    lax.fori_loop(1, PLANE, greet, 0)

    def greet_z(step, carry):
        pl.semaphore_signal(barrier, inc=1, device_id=(p, lax.rem(z + step, SIDE)), device_id_type=MESH)
        return carry

    lax.fori_loop(1, SIDE, greet_z, 0)
    pl.semaphore_wait(barrier, PLANE - 1 + SIDE - 1)

    def a_rows(source_chip, source_core):
        return pl.ds(pl.multiple_of((2 * source_chip + source_core) * rows, rows), rows)

    def a_piece(offset, i):
        at_x, at_y = place(offset)
        return amp.at[at_y * per_i + i, :, :, pl.ds(pl.multiple_of(at_x * per_b, per_b), per_b)]

    def a_lanes(i):
        return pl.ds(i * per_b, per_b)

    for m, (dest, via) in enumerate(RELAYED):
        for i in range(per_i):
            remote(
                a_piece(dest, i), a_relay.at[m, :, :, a_lanes(i)], s1.at[m], rr.at[m], (2 * chip_at(via) + core, z)
            ).start()
    for n, dest in enumerate(DIRECT):
        for i in range(per_i):
            remote(
                a_piece(dest, i), a_all.at[:, a_rows(chip, core), a_lanes(i)], s1.at[len(RELAYED) + n], r1.at[chip],
                (2 * chip_at(dest) + core, z),
            ).start()
    for i in range(per_i):
        pltpu.make_async_copy(a_piece((0, 0), i), a_all.at[:, a_rows(chip, core), a_lanes(i)], r1.at[chip]).start()

    @pl.when(p == 0)
    def _():
        load_h.wait()
        flat = head_v[...].reshape(pairs * 16, n_b)
        r = lax.broadcasted_iota(jnp.int32, (pairs, pairs * 16), 0)
        c = lax.broadcasted_iota(jnp.int32, (pairs, pairs * 16), 1)
        for t in range(4):
            pick = jnp.where(c == 16 * r + t, 1.0, 0.0).astype(BF16)
            one = jnp.dot(pick, flat, preferred_element_type=F32).astype(BF16)
            for zz in range(SIDE):
                tile_out[zz, t] = one[:, zz * per_b : (zz + 1) * per_b]
        pltpu.make_async_copy(tile_out.at[z], tile_in.at[z], tz_recv.at[z]).start()

        def send_t(step, carry):
            zz = lax.rem(z + step, SIDE)
            remote(tile_out.at[zz], tile_in.at[z], tz_send.at[zz], tz_recv.at[z], (p, zz)).start()
            return carry

        lax.fori_loop(1, SIDE, send_t, 0)

    load_w.wait()
    r = lax.broadcasted_iota(jnp.int32, (256, 128), 0)
    c = lax.broadcasted_iota(jnp.int32, (256, 128), 1)
    pick = jnp.where(r == 2 * c + core, 1.0, 0.0).astype(BF16)
    for k in range(n_k):

        def prep(block, carry):
            at = pl.multiple_of(block * 128, 128)
            both = wraw_v[k, pl.ds(at, 128), :, :].reshape(256, per_b)
            turned = lax.dot_general(both, pick, (((0,), (0,)), ((), ())), preferred_element_type=F32)
            turned = turned.astype(BF16)
            for g in range(per_b // GROUP):
                wt[z, g % CHUNKS, g // CHUNKS, :, pl.ds(pl.multiple_of(k * n_c + at, 128), 128)] = turned[
                    g * GROUP : (g + 1) * GROUP
                ]
            return carry

        lax.fori_loop(0, n_c // 128, prep, 0, unroll=2)

    def w_own(g, way):
        ref = wt.at[z, g // 2, pl.ds(4 * (g % 2), 4)]
        return remote(ref, ref, wsend.at[way, g], wrecv.at[way, g], neighbour[way])

    def w_half(g, way):
        return pl.ds(4 * (g % 2) + 2 * way, 2)

    def w_start(g):
        for way in range(2):
            w_own(g, way).start()

    def w_pass(g):
        for way in range(2):
            await_bytes(wt.at[z_source[way], g // 2, pl.ds(4 * (g % 2), 4)], wrecv.at[way, g])
            ref = wt.at[z_source[way], g // 2, w_half(g, way)]
            remote(ref, ref, wfsend.at[way, g], wfrecv.at[way, g], neighbour[way]).start()

    def w_far(g):
        for way in range(2):
            await_bytes(wt.at[z_far, g // 2, w_half(g, way)], wfrecv.at[way, g])

    w_start(0)
    w_start(1)

    for m, (dest, via) in enumerate(RELAYED):
        await_bytes(a_relay.at[m], rr.at[m])
        source = chip_at(back(via))
        remote(
            a_relay.at[m], a_all.at[:, a_rows(source, core), :], rs.at[m], r1.at[source],
            (2 * chip_at(beyond(dest, via)) + core, z),
        ).start()

    def pass_a(offsets):
        for offset in offsets:
            source = chip_at(back(offset))
            ref = a_all.at[:, a_rows(source, core), :]
            await_bytes(ref, r1.at[source])
            remote(ref, ref, sf.at[source], rf.at[source], partner).start()

    def tile_down():
        for dy in range(1, SIDE):
            remote(tile_in, tile_in, tb_send.at[dy + 2], tb_recv, (2 * (dy * SIDE + x), z)).start()
        remote(tile_in, tile_in, tf_send, tb_recv, partner).start()

    @pl.when(p == 0)
    def _():
        for zz in range(SIDE):
            await_bytes(tile_in.at[zz], tz_recv.at[zz])
        for dx in range(1, SIDE):
            remote(tile_in, tile_in, tb_send.at[dx - 1], tb_recv, (2 * dx, z)).start()
        tile_down()

    pass_a(((0, 0),) + DIRECT[:4])
    w_pass(0)
    w_start(2)

    @pl.when((y == 0) & (core == 0) & (x != 0))
    def _():
        await_bytes(tile_in, tb_recv)
        tile_down()

    pass_a(DIRECT[4:])
    w_pass(1)
    w_start(3)

    @pl.when((y != 0) & (core == 0))
    def _():
        await_bytes(tile_in, tb_recv)
        remote(tile_in, tile_in, tf_send, tb_recv, partner).start()

    pass_a([dest for dest, _ in RELAYED])
    w_pass(2)
    w_start(4)

    def got_a(source, carry):
        await_bytes(a_all.at[:, a_rows(source, 1 - core), :], rf.at[source])
        return carry

    lax.fori_loop(0, CHIPS, got_a, 0)

    def target(at_x, at_y, t):
        return coupled.at[
            pl.ds(at_y * per_i, per_i), core, pl.ds(t * GROUP, GROUP),
            pl.ds(pl.multiple_of(at_x * per_b, per_b), per_b),
        ]

    def product(t):
        left = wt[:, t].reshape(PLANE * GROUP, depth)
        for start, size in ((0, 512), (512, 512), (1024, 128)):
            right = a_all[:, :, start : start + size].reshape(depth, size)
            value = jnp.dot(left, right, preferred_element_type=F32).astype(BF16)
            for lane in range(0, size, 128):
                i, at = (start + lane) // per_b, (start + lane) % per_b
                prod[t, :, i, :, at : at + 128] = value[:, lane : lane + 128].reshape(PLANE, GROUP, 128)
        for m, (dest, via) in enumerate(RELAYED):
            remote(
                prod.at[t, pl.ds(2 * chip_at(dest), 2)], c_relay.at[t, m], csend.at[t], crr.at[t, m],
                (2 * chip_at(via) + core, z),
            ).start()
        here = target(x, y, t)
        for dest in DIRECT:
            for other in range(2):
                q = 2 * chip_at(dest) + other
                remote(prod.at[t, q], here, csend.at[t], crecv, (q, z)).start()
        remote(prod.at[t, partner[0]], here, csend.at[t], crecv, partner).start()
        pltpu.make_async_copy(prod.at[t, p], here, crecv).start()

    def pass_c(t):
        for m, (dest, via) in enumerate(RELAYED):
            await_bytes(c_relay.at[t, m], crr.at[t, m])
            at_x, at_y = place(back(via))
            for other in range(2):
                q = 2 * chip_at(beyond(dest, via)) + other
                remote(c_relay.at[t, m, other], target(at_x, at_y, t), crs.at[t], crecv, (q, z)).start()

    w_far(0)
    w_far(1)
    product(0)

    @pl.when(core == 1)
    def _():
        await_bytes(tile_in, tb_recv)

    load_v.wait()
    for zz in range(SIDE):
        total = None
        for t in range(4):
            right = v_v[:, t].reshape(4 * rows, per_b)
            term = lax.dot_general(
                tile_in[zz, t], right, (((1,), (1,)), ((), ())), preferred_element_type=F32
            )
            total = term if total is None else total + term
        part[zz] = total
    pltpu.make_async_copy(part.at[z], part_in.at[z], p_recv.at[z]).start()

    def send_p(step, carry):
        zz = lax.rem(z + step, SIDE)
        remote(part.at[zz], part_in.at[z], p_send.at[zz], p_recv.at[z], (p, zz)).start()
        return carry

    lax.fori_loop(1, SIDE, send_p, 0)
    w_pass(3)
    w_start(5)
    pass_c(0)

    row = lax.broadcasted_iota(jnp.int32, (rows, n_b), 0)
    col = lax.broadcasted_iota(jnp.int32, (rows, n_b), 1)
    mine = col == row + p * rows
    energy = jnp.broadcast_to(virt_e[...].reshape(1, n_b), (rows, n_b))
    table[0] = energy + jnp.sum(jnp.where(mine, energy, 0.0), axis=1, keepdims=True)
    blocks = virt_l.shape[1]
    first = lax.broadcasted_iota(jnp.int32, (blocks, n_b), 0) * VBLK
    at = lax.broadcasted_iota(jnp.int32, (blocks, n_b), 1)
    member = jnp.where((at >= first) & (at < first + VBLK), 1.0, 0.0).astype(BF16)
    labels = jnp.broadcast_to((virt_l[...] & 1).astype(F32).astype(BF16), (8, blocks))
    label = jnp.dot(labels, member, preferred_element_type=F32)
    label = jnp.broadcast_to(label[0:1], (rows, n_b))
    table[1] = jnp.abs(label - jnp.sum(jnp.where(mine, label, 0.0), axis=1, keepdims=True))
    pltpu.make_async_copy(table, table_out, load_sem.at[0]).start()

    for zz in range(SIDE):
        await_bytes(part_in.at[zz], p_recv.at[zz])
    sum_v[...] = part_in[0] + part_in[1] + part_in[2] + part_in[3]

    @pl.when(p == 0)
    def _():
        pltpu.make_async_copy(sum_v, fin_in.at[0], f_recv).start()

    @pl.when(p != 0)
    def _():
        remote(sum_v, fin_in.at[p], f_send, f_recv, (0, z)).start()

    w_pass(4)
    w_far(2)
    w_far(3)
    product(1)
    w_pass(5)
    pass_c(1)

    @pl.when(p == 0)
    def _():
        await_bytes(fin_in, f_recv)
        for q in range(PLANE):
            for a in range(4):
                lad_v[a, :, q * rows : (q + 1) * rows] = fin_in[q, :, a * rows : (a + 1) * rows]
        pltpu.make_async_copy(lad_v, lad_out, load_sem.at[2]).start()

    w_far(4)
    w_far(5)
    product(2)
    pass_c(2)

    one_a = a_all.at[:, pl.ds(0, rows), :]
    for n in range(CHIPS - 1):
        await_bytes(one_a, s1.at[n])
    for m in range(len(RELAYED)):
        await_bytes(a_relay.at[m], rs.at[m])

    def passed_a(step, carry):
        await_bytes(a_all.at[:, a_rows(step, core), :], sf.at[step])
        return carry

    lax.fori_loop(0, CHIPS, passed_a, 0)
    for way in range(2):
        for g in range(PARTS):
            await_bytes(wt.at[z, g // 2, pl.ds(4 * (g % 2), 4)], wsend.at[way, g])
            await_bytes(wt.at[z, g // 2, w_half(g, way)], wfsend.at[way, g])

    def sent_p(step, carry):
        zz = lax.rem(z + step, SIDE)
        await_bytes(part.at[zz], p_send.at[zz])
        return carry

    lax.fori_loop(1, SIDE, sent_p, 0)

    @pl.when(core == 0)
    def _():
        await_bytes(tile_in, tf_send)

    @pl.when((y == 0) & (core == 0))
    def _():
        for dy in range(1, SIDE):
            await_bytes(tile_in, tb_send.at[dy + 2])

    @pl.when(p == 0)
    def _():
        def sent_t(step, carry):
            zz = lax.rem(z + step, SIDE)
            await_bytes(tile_out.at[zz], tz_send.at[zz])
            return carry

        lax.fori_loop(1, SIDE, sent_t, 0)
        for dx in range(1, SIDE):
            await_bytes(tile_in, tb_send.at[dx - 1])
        await_bytes(lad_v, load_sem.at[2])

    @pl.when(p != 0)
    def _():
        await_bytes(sum_v, f_send)

    await_bytes(table, load_sem.at[0])
    for t in range(CHUNKS):
        await_bytes(prod.at[t, pl.ds(0, PLANE - 1)], csend.at[t])
        await_bytes(c_relay.at[t], crs.at[t])
    await_bytes(coupled, crecv)


def exchange(amp, wraw, vint, virt_e, virt_l):
    n_i, n_k, rows, n_b = amp.shape
    per_i, per_b, n_c = n_i // SIDE, n_b // SIDE, rows * PLANE
    pairs, relays = n_i * n_k, len(RELAYED)
    dma = pltpu.SemaphoreType.DMA
    anywhere = pl.BlockSpec(memory_space=pl.ANY)
    inside = pl.BlockSpec(memory_space=pltpu.VMEM)
    return pl.pallas_call(
        exchange_kernel,
        out_shape=(
            jax.ShapeDtypeStruct(amp.shape, BF16),
            jax.ShapeDtypeStruct((4, pairs, n_b), F32),
            jax.ShapeDtypeStruct((2, rows, n_b), F32),
        ),
        in_specs=[anywhere] * 3 + [inside] * 2,
        out_specs=(anywhere,) * 3,
        scratch_shapes=[
            pltpu.VMEM(wraw.shape, BF16),
            pltpu.VMEM(vint.shape, BF16),
            pltpu.VMEM((n_i, n_k, 16, n_b), BF16),
            pltpu.VMEM((SIDE, CHUNKS, 8, GROUP, n_k * n_c), BF16),
            pltpu.VMEM((n_k, n_c, per_i * per_b), BF16),
            pltpu.VMEM((CHUNKS, PLANE, per_i, GROUP, per_b), BF16),
            pltpu.VMEM((relays, n_k, rows, per_i * per_b), BF16),
            pltpu.VMEM((CHUNKS, relays, 2, per_i, GROUP, per_b), BF16),
            pltpu.VMEM((SIDE, 4, pairs, per_b), BF16),
            pltpu.VMEM((SIDE, 4, pairs, per_b), BF16),
            pltpu.VMEM((SIDE, pairs, 4 * rows), F32),
            pltpu.VMEM((SIDE, pairs, 4 * rows), F32),
            pltpu.VMEM((pairs, 4 * rows), F32),
            pltpu.VMEM((PLANE, pairs, 4 * rows), F32),
            pltpu.VMEM((4, pairs, n_b), F32),
            pltpu.VMEM((2, rows, n_b), F32),
            dma((3,)),
            dma((CHIPS - 1,)),
            dma((CHIPS,)),
            dma((relays,)),
            dma((relays,)),
            dma((CHIPS,)),
            dma((CHIPS,)),
            dma((2, PARTS)),
            dma((2, PARTS)),
            dma((2, PARTS)),
            dma((2, PARTS)),
            dma((CHUNKS,)),
            dma,
            dma((CHUNKS,)),
            dma((CHUNKS, relays)),
            dma((SIDE,)),
            dma((SIDE,)),
            dma((6,)),
            dma,
            dma,
            dma((SIDE,)),
            dma((SIDE,)),
            dma,
            dma,
        ],
        compiler_params=pltpu.CompilerParams(
            collective_id=0, has_side_effects=True, vmem_limit_bytes=60 * 1024 * 1024
        ),
        name="exchange",
    )(amp, wraw, vint, virt_e, virt_l.reshape(1, -1))


def update_kernel(coupled, pair, lad, table, occ_e, occ_l, slab_i, slab_j, out):
    p = lax.axis_index("wide")
    step = pl.program_id(0)
    rows, n_b = table.shape[1:]
    energy_i = occ_e[slab_i[step]]
    label_i = occ_l[slab_i[step]]
    for j in range(coupled.shape[1]):
        energy = energy_i + occ_e[slab_j[j]]
        odd = ((label_i + occ_l[slab_j[j]]) & 1).astype(F32)

        def update(value, count):
            residual = pair[0, j, 0:count].astype(F32) + value
            allowed = (1.0 - odd) + (2.0 * odd - 1.0) * table[1, 0:count]
            return (allowed * residual / (table[0, 0:count] - energy)).astype(BF16)

        out[0, j] = update(coupled[0, j].astype(F32), rows)

        @pl.when(p == 0)
        def _():
            at = step * coupled.shape[1] + j
            term = jnp.concatenate(
                [lad[a, pl.ds(at, 1), :] for a in range(4)] + [jnp.zeros((12, n_b), F32)], axis=0
            )
            value = (coupled[0, j, 0:16].astype(F32) + term).astype(BF16).astype(F32)
            out[0, j, 0:16] = update(value, 16)


def denominator_update(coupled, pair, lad, table, occ_e, occ_l, slab_i, slab_j):
    n_i, n_j, rows, n_b = pair.shape
    block = pl.BlockSpec((1, n_j, rows, n_b), lambda i: (i, 0, 0, 0))
    scalars = pl.BlockSpec(memory_space=pltpu.SMEM)
    return pl.pallas_call(
        update_kernel,
        grid=(n_i,),
        out_shape=jax.ShapeDtypeStruct(pair.shape, BF16),
        in_specs=[
            block,
            block,
            pl.BlockSpec(lad.shape, lambda i: (0, 0, 0)),
            pl.BlockSpec(table.shape, lambda i: (0, 0, 0)),
            scalars,
            scalars,
            scalars,
            scalars,
        ],
        out_specs=block,
        name="update",
    )(coupled, pair, lad, table, occ_e, occ_l, slab_i, slab_j)


def per_device(
    amplitudes,
    pair_integrals,
    cycle_integrals,
    ladder_integrals,
    occ_energy,
    virt_energy,
    occ_irrep,
    virt_irrep,
    slab_i,
    slab_j,
):
    coupled, lad, table = exchange(amplitudes, cycle_integrals, ladder_integrals, virt_energy, virt_irrep)
    return denominator_update(coupled, pair_integrals, lad, table, occ_energy, occ_irrep, slab_i, slab_j)


def solution(mesh):
    return jax.shard_map(
        per_device,
        mesh=mesh,
        in_specs=(
            P("narrow", None, "wide", None),
            P("narrow", None, "wide", None),
            P(None, None, None, "narrow"),
            P(None, None, "wide", "narrow"),
            P(),
            P(),
            P(),
            P(),
            P("narrow"),
            P(),
        ),
        out_specs=P("narrow", None, "wide", None),
        check_vma=False,
    )
```

```python
import jax
import jax.numpy as jnp
from jax import lax
from jax.experimental import pallas as pl
from jax.experimental.pallas import tpu as pltpu
from jax.sharding import PartitionSpec as P

MESH = pl.DeviceIdType.MESH
BF16 = jnp.bfloat16
F32 = jnp.float32
VBLK = 16
SIDE = 4
CHIPS = SIDE * SIDE
PLANE = 2 * CHIPS
GROUP = 16
PARTS = 6
DIRECT = ((1, 0), (3, 0), (0, 1), (0, 3), (1, 1), (1, 3), (3, 1), (3, 3), (2, 0), (0, 2), (2, 2))
RELAYED = (((2, 1), (3, 0)), ((2, 3), (3, 0)), ((1, 2), (1, 3)), ((3, 2), (3, 3)))


def remote(src, dst, send_sem, recv_sem, device):
    return pltpu.make_async_remote_copy(
        src_ref=src, dst_ref=dst, send_sem=send_sem, recv_sem=recv_sem, device_id=device, device_id_type=MESH
    )


def await_bytes(ref, sem):
    pltpu.make_async_copy(ref, ref, sem).wait()


def exchange_kernel(
    amp, wraw, vint, virt_e, virt_l, coupled, lad_out, table_out,
    wraw_v, v_v, head_v, wt, a_all, prod, a_relay, c_relay, tile_out, tile_in, part, part_in, sum_v, fin_in, lad_v, table,
    load_sem, s1, r1, rs, rr, sf, rf, wsend, wrecv, wfsend, wfrecv, csend, cpsend, crecv, crs, crr,
    tz_send, tz_recv, tb_send, tb_recv, tf_send, p_send, p_recv, f_send, f_recv,
):
    p = lax.axis_index("wide")
    z = lax.axis_index("narrow")
    core = lax.rem(p, 2)
    chip = lax.div(p, 2)
    x = lax.rem(chip, SIDE)
    y = lax.div(chip, SIDE)
    partner = (p + 1 - 2 * core, z)
    z_up = lax.rem(z + 1, SIDE)
    z_down = lax.rem(z + SIDE - 1, SIDE)
    z_far = lax.rem(z + 2, SIDE)
    neighbour = ((p, z_up), (p, z_down))
    z_source = (z_down, z_up)
    n_i, n_k, rows, n_b = amp.shape
    per_i = n_i // SIDE
    per_b = n_b // SIDE
    n_c = rows * PLANE
    depth = n_k * n_c
    pairs = n_i * n_k

    def place(offset):
        return lax.rem(x + offset[0] + SIDE, SIDE), lax.rem(y + offset[1] + SIDE, SIDE)

    def chip_at(offset):
        at_x, at_y = place(offset)
        return at_y * SIDE + at_x

    def back(offset):
        return (-offset[0], -offset[1])

    def beyond(dest, via):
        return ((dest[0] - via[0]) % SIDE, (dest[1] - via[1]) % SIDE)

    load_w = pltpu.make_async_copy(wraw, wraw_v, load_sem.at[0])
    load_v = pltpu.make_async_copy(vint, v_v, load_sem.at[1])
    load_h = pltpu.make_async_copy(amp.at[:, :, pl.ds(0, 16), :], head_v, load_sem.at[2])
    load_w.start()
    load_v.start()

    @pl.when(p == 0)
    def _():
        load_h.start()

    barrier = pltpu.get_barrier_semaphore()

    def greet(step, carry):
        pl.semaphore_signal(barrier, inc=1, device_id=(lax.rem(p + step, PLANE), z), device_id_type=MESH)
        return carry

    lax.fori_loop(1, PLANE, greet, 0)

    def greet_z(step, carry):
        pl.semaphore_signal(barrier, inc=1, device_id=(p, lax.rem(z + step, SIDE)), device_id_type=MESH)
        return carry

    lax.fori_loop(1, SIDE, greet_z, 0)

    load_w.wait()
    r = lax.broadcasted_iota(jnp.int32, (256, 128), 0)
    c = lax.broadcasted_iota(jnp.int32, (256, 128), 1)
    pick = jnp.where(r == 2 * c + core, 1.0, 0.0).astype(BF16)
    groups = 128 // GROUP

    def owner_of(n):
        first, owner = n * GROUP % rows // GROUP, n * GROUP // rows
        return 2 * first + owner % 2, owner // 2

    def prep(lane):
        for k in range(n_k):

            def turn(block, carry):
                at = pl.multiple_of(block * 128, 128)
                both = wraw_v[k, pl.ds(at, 128), :, lane * 128 : (lane + 1) * 128].reshape(256, 128)
                turned = lax.dot_general(both, pick, (((0,), (0,)), ((), ())), preferred_element_type=F32)
                turned = turned.astype(BF16)
                for n in range(groups):
                    g, owner_x = owner_of(lane * groups + n)
                    wt[z, g, owner_x, :, pl.ds(pl.multiple_of(k * n_c + at, 128), 128)] = turned[
                        n * GROUP : (n + 1) * GROUP
                    ]
                return carry

            lax.fori_loop(0, n_c // 128, turn, 0, unroll=4)

    def w_copy(ref, g, way):
        return remote(ref, ref, wsend.at[way, g], wrecv.at[way, g], neighbour[way])

    def w_early(lane):
        for n in range(lane * groups, (lane + 1) * groups):
            g, owner_x = owner_of(n)
            if g < 2:
                for way in range(2):
                    w_copy(wt.at[z, g, owner_x], g, way).start()

    prep(0)
    pl.semaphore_wait(barrier, PLANE - 1 + SIDE - 1)
    w_early(0)

    def a_rows(source_chip, source_core):
        return pl.ds(pl.multiple_of((2 * source_chip + source_core) * rows, rows), rows)

    def a_piece(offset, i):
        at_x, at_y = place(offset)
        return amp.at[at_y * per_i + i, :, :, pl.ds(pl.multiple_of(at_x * per_b, per_b), per_b)]

    def a_lanes(i):
        return pl.ds(i * per_b, per_b)

    for m, (dest, via) in enumerate(RELAYED):
        for i in range(per_i):
            remote(
                a_piece(dest, i), a_relay.at[m, :, :, a_lanes(i)], s1.at[m], rr.at[m], (2 * chip_at(via) + core, z)
            ).start()
    for n, dest in enumerate(DIRECT):
        for i in range(per_i):
            remote(
                a_piece(dest, i), a_all.at[:, a_rows(chip, core), a_lanes(i)], s1.at[len(RELAYED) + n], r1.at[chip],
                (2 * chip_at(dest) + core, z),
            ).start()
    for i in range(per_i):
        pltpu.make_async_copy(a_piece((0, 0), i), a_all.at[:, a_rows(chip, core), a_lanes(i)], r1.at[chip]).start()

    @pl.when(p == 0)
    def _():
        load_h.wait()
        flat = head_v[...].reshape(pairs * 16, n_b)
        r = lax.broadcasted_iota(jnp.int32, (pairs, pairs * 16), 0)
        c = lax.broadcasted_iota(jnp.int32, (pairs, pairs * 16), 1)
        for t in range(4):
            pick = jnp.where(c == 16 * r + t, 1.0, 0.0).astype(BF16)
            one = jnp.dot(pick, flat, preferred_element_type=F32).astype(BF16)
            for zz in range(SIDE):
                tile_out[zz, t] = one[:, zz * per_b : (zz + 1) * per_b]
        pltpu.make_async_copy(tile_out.at[z], tile_in.at[z], tz_recv.at[z]).start()

        def send_t(step, carry):
            zz = lax.rem(z + step, SIDE)
            remote(tile_out.at[zz], tile_in.at[z], tz_send.at[zz], tz_recv.at[z], (p, zz)).start()
            return carry

        lax.fori_loop(1, SIDE, send_t, 0)

    for lane in range(1, per_b // 128):
        prep(lane)
        w_early(lane)

    def w_start(g):
        for way in range(2):
            w_copy(wt.at[z, g], g, way).start()

    def w_half(source, g, way):
        return wt.at[source, g, pl.ds(2 * way, 2)]

    def w_pass(g):
        for way in range(2):
            await_bytes(wt.at[z_source[way], g], wrecv.at[way, g])
            ref = w_half(z_source[way], g, way)
            remote(ref, ref, wfsend.at[way, g], wfrecv.at[way, g], neighbour[way]).start()

    def w_far(g):
        for way in range(2):
            await_bytes(w_half(z_far, g, way), wfrecv.at[way, g])

    for m, (dest, via) in enumerate(RELAYED):
        await_bytes(a_relay.at[m], rr.at[m])
        source = chip_at(back(via))
        remote(
            a_relay.at[m], a_all.at[:, a_rows(source, core), :], rs.at[m], r1.at[source],
            (2 * chip_at(beyond(dest, via)) + core, z),
        ).start()

    def pass_a(offsets):
        for offset in offsets:
            source = chip_at(back(offset))
            ref = a_all.at[:, a_rows(source, core), :]
            await_bytes(ref, r1.at[source])
            remote(ref, ref, sf.at[source], rf.at[source], partner).start()

    def tile_down():
        for dy in range(1, SIDE):
            remote(tile_in, tile_in, tb_send.at[dy + 2], tb_recv, (2 * (dy * SIDE + x), z)).start()
        remote(tile_in, tile_in, tf_send, tb_recv, partner).start()

    @pl.when(p == 0)
    def _():
        for zz in range(SIDE):
            await_bytes(tile_in.at[zz], tz_recv.at[zz])
        for dx in range(1, SIDE):
            remote(tile_in, tile_in, tb_send.at[dx - 1], tb_recv, (2 * dx, z)).start()
        tile_down()

    pass_a(((0, 0),) + DIRECT[:4])
    w_pass(0)
    w_start(2)

    @pl.when((y == 0) & (core == 0) & (x != 0))
    def _():
        await_bytes(tile_in, tb_recv)
        tile_down()

    pass_a(DIRECT[4:8])
    w_pass(1)
    w_start(3)

    @pl.when((y != 0) & (core == 0))
    def _():
        await_bytes(tile_in, tb_recv)
        remote(tile_in, tile_in, tf_send, tb_recv, partner).start()

    pass_a(DIRECT[8:] + tuple(dest for dest, _ in RELAYED))
    w_pass(2)
    w_start(4)

    def got_a(source, carry):
        await_bytes(a_all.at[:, a_rows(source, 1 - core), :], rf.at[source])
        return carry

    lax.fori_loop(0, CHIPS, got_a, 0)

    def target(at_x, at_y, t, i=None):
        at_i = pl.ds(at_y * per_i, per_i) if i is None else at_y * per_i + i
        return coupled.at[at_i, core, pl.ds(t * GROUP, GROUP), pl.ds(pl.multiple_of(at_x * per_b, per_b), per_b)]

    def send_c(g, i=None):
        t, owner_core = g // 2, g % 2

        def one(ref, *index):
            return ref.at[index] if i is None else ref.at[index + (i,)]

        here = target(x, y, t, i)
        for m, (dest, via) in enumerate(RELAYED):
            remote(
                one(prod, g, chip_at(dest)), one(c_relay, g, m), csend.at[g], crr.at[g, m],
                (2 * chip_at(via) + core, z),
            ).start()
        for dest in DIRECT:
            remote(
                one(prod, g, chip_at(dest)), here, csend.at[g], crecv, (2 * chip_at(dest) + owner_core, z)
            ).start()

    def product(g):
        left = wt[:, g].reshape(CHIPS * GROUP, depth)

        def columns(start, size):
            right = a_all[:, :, start : start + size].reshape(depth, size)
            value = jnp.dot(left, right, preferred_element_type=F32).astype(BF16)
            for lane in range(0, size, 128):
                i, at = (start + lane) // per_b, (start + lane) % per_b
                prod[g, :, i, :, at : at + 128] = value[:, lane : lane + 128].reshape(CHIPS, GROUP, 128)

        if g == PARTS - 1:
            for i in range(per_i):
                columns(i * per_b, per_b)
                send_c(g, i)
        else:
            columns(0, per_i * per_b)
            send_c(g)
        if g % 2 == 1:
            t = g // 2
            here = target(x, y, t)
            remote(prod.at[2 * t + 1 - core, chip], here, cpsend.at[t], crecv, partner).start()
            pltpu.make_async_copy(prod.at[2 * t + core, chip], here, crecv).start()

    def pass_c(g):
        for m, (dest, via) in enumerate(RELAYED):
            await_bytes(c_relay.at[g, m], crr.at[g, m])
            at_x, at_y = place(back(via))
            owner = 2 * chip_at(beyond(dest, via)) + g % 2
            remote(c_relay.at[g, m], target(at_x, at_y, g // 2), crs.at[g], crecv, (owner, z)).start()

    w_far(0)
    product(0)
    w_far(1)
    product(1)

    @pl.when(core == 1)
    def _():
        await_bytes(tile_in, tb_recv)

    load_v.wait()
    for zz in range(SIDE):
        total = None
        for t in range(4):
            right = v_v[:, t].reshape(4 * rows, per_b)
            term = lax.dot_general(
                tile_in[zz, t], right, (((1,), (1,)), ((), ())), preferred_element_type=F32
            )
            total = term if total is None else total + term
        part[zz] = total
    pltpu.make_async_copy(part.at[z], part_in.at[z], p_recv.at[z]).start()

    def send_p(step, carry):
        zz = lax.rem(z + step, SIDE)
        remote(part.at[zz], part_in.at[z], p_send.at[zz], p_recv.at[z], (p, zz)).start()
        return carry

    lax.fori_loop(1, SIDE, send_p, 0)
    w_pass(3)
    w_start(5)
    pass_c(0)
    pass_c(1)
    w_far(2)
    product(2)
    w_pass(4)
    pass_c(2)

    row = lax.broadcasted_iota(jnp.int32, (rows, n_b), 0)
    col = lax.broadcasted_iota(jnp.int32, (rows, n_b), 1)
    mine = col == row + p * rows
    energy = jnp.broadcast_to(virt_e[...].reshape(1, n_b), (rows, n_b))
    table[0] = energy + jnp.sum(jnp.where(mine, energy, 0.0), axis=1, keepdims=True)
    blocks = virt_l.shape[1]
    first = lax.broadcasted_iota(jnp.int32, (blocks, n_b), 0) * VBLK
    at = lax.broadcasted_iota(jnp.int32, (blocks, n_b), 1)
    member = jnp.where((at >= first) & (at < first + VBLK), 1.0, 0.0).astype(BF16)
    labels = jnp.broadcast_to((virt_l[...] & 1).astype(F32).astype(BF16), (8, blocks))
    label = jnp.dot(labels, member, preferred_element_type=F32)
    label = jnp.broadcast_to(label[0:1], (rows, n_b))
    table[1] = jnp.abs(label - jnp.sum(jnp.where(mine, label, 0.0), axis=1, keepdims=True))
    pltpu.make_async_copy(table, table_out, load_sem.at[0]).start()

    for zz in range(SIDE):
        await_bytes(part_in.at[zz], p_recv.at[zz])
    sum_v[...] = part_in[0] + part_in[1] + part_in[2] + part_in[3]

    @pl.when(p == 0)
    def _():
        pltpu.make_async_copy(sum_v, fin_in.at[0], f_recv).start()

    @pl.when(p != 0)
    def _():
        remote(sum_v, fin_in.at[p], f_send, f_recv, (0, z)).start()

    w_far(3)
    product(3)
    w_pass(5)
    pass_c(3)

    @pl.when(p == 0)
    def _():
        await_bytes(fin_in, f_recv)
        for q in range(PLANE):
            for a in range(4):
                lad_v[a, :, q * rows : (q + 1) * rows] = fin_in[q, :, a * rows : (a + 1) * rows]
        pltpu.make_async_copy(lad_v, lad_out, load_sem.at[2]).start()

    w_far(4)
    product(4)
    w_far(5)
    product(5)
    pass_c(4)
    pass_c(5)

    one_a = a_all.at[:, pl.ds(0, rows), :]
    for n in range(CHIPS - 1):
        await_bytes(one_a, s1.at[n])
    for m in range(len(RELAYED)):
        await_bytes(a_relay.at[m], rs.at[m])

    def passed_a(step, carry):
        await_bytes(a_all.at[:, a_rows(step, core), :], sf.at[step])
        return carry

    lax.fori_loop(0, CHIPS, passed_a, 0)
    for way in range(2):
        for g in range(PARTS):
            await_bytes(wt.at[z, g], wsend.at[way, g])
            await_bytes(w_half(z, g, way), wfsend.at[way, g])

    def sent_p(step, carry):
        zz = lax.rem(z + step, SIDE)
        await_bytes(part.at[zz], p_send.at[zz])
        return carry

    lax.fori_loop(1, SIDE, sent_p, 0)

    @pl.when(core == 0)
    def _():
        await_bytes(tile_in, tf_send)

    @pl.when((y == 0) & (core == 0))
    def _():
        for dy in range(1, SIDE):
            await_bytes(tile_in, tb_send.at[dy + 2])

    @pl.when(p == 0)
    def _():
        def sent_t(step, carry):
            zz = lax.rem(z + step, SIDE)
            await_bytes(tile_out.at[zz], tz_send.at[zz])
            return carry

        lax.fori_loop(1, SIDE, sent_t, 0)
        for dx in range(1, SIDE):
            await_bytes(tile_in, tb_send.at[dx - 1])
        await_bytes(lad_v, load_sem.at[2])

    @pl.when(p != 0)
    def _():
        await_bytes(sum_v, f_send)

    await_bytes(table, load_sem.at[0])
    for g in range(PARTS):
        await_bytes(prod.at[g, pl.ds(0, CHIPS - 1)], csend.at[g])
        await_bytes(c_relay.at[g], crs.at[g])
    for t in range(PARTS // 2):
        await_bytes(prod.at[t, 0], cpsend.at[t])
    await_bytes(coupled, crecv)


def exchange(amp, wraw, vint, virt_e, virt_l):
    n_i, n_k, rows, n_b = amp.shape
    per_i, per_b, n_c = n_i // SIDE, n_b // SIDE, rows * PLANE
    pairs, relays = n_i * n_k, len(RELAYED)
    dma = pltpu.SemaphoreType.DMA
    anywhere = pl.BlockSpec(memory_space=pl.ANY)
    inside = pl.BlockSpec(memory_space=pltpu.VMEM)
    return pl.pallas_call(
        exchange_kernel,
        out_shape=(
            jax.ShapeDtypeStruct(amp.shape, BF16),
            jax.ShapeDtypeStruct((4, pairs, n_b), F32),
            jax.ShapeDtypeStruct((2, rows, n_b), F32),
        ),
        in_specs=[anywhere] * 3 + [inside] * 2,
        out_specs=(anywhere,) * 3,
        scratch_shapes=[
            pltpu.VMEM(wraw.shape, BF16),
            pltpu.VMEM(vint.shape, BF16),
            pltpu.VMEM((n_i, n_k, 16, n_b), BF16),
            pltpu.VMEM((SIDE, PARTS, SIDE, GROUP, n_k * n_c), BF16),
            pltpu.VMEM((n_k, n_c, per_i * per_b), BF16),
            pltpu.VMEM((PARTS, CHIPS, per_i, GROUP, per_b), BF16),
            pltpu.VMEM((relays, n_k, rows, per_i * per_b), BF16),
            pltpu.VMEM((PARTS, relays, per_i, GROUP, per_b), BF16),
            pltpu.VMEM((SIDE, 4, pairs, per_b), BF16),
            pltpu.VMEM((SIDE, 4, pairs, per_b), BF16),
            pltpu.VMEM((SIDE, pairs, 4 * rows), F32),
            pltpu.VMEM((SIDE, pairs, 4 * rows), F32),
            pltpu.VMEM((pairs, 4 * rows), F32),
            pltpu.VMEM((PLANE, pairs, 4 * rows), F32),
            pltpu.VMEM((4, pairs, n_b), F32),
            pltpu.VMEM((2, rows, n_b), F32),
            dma((3,)),
            dma((CHIPS - 1,)),
            dma((CHIPS,)),
            dma((relays,)),
            dma((relays,)),
            dma((CHIPS,)),
            dma((CHIPS,)),
            dma((2, PARTS)),
            dma((2, PARTS)),
            dma((2, PARTS)),
            dma((2, PARTS)),
            dma((PARTS,)),
            dma((PARTS // 2,)),
            dma,
            dma((PARTS,)),
            dma((PARTS, relays)),
            dma((SIDE,)),
            dma((SIDE,)),
            dma((6,)),
            dma,
            dma,
            dma((SIDE,)),
            dma((SIDE,)),
            dma,
            dma,
        ],
        compiler_params=pltpu.CompilerParams(
            collective_id=0, has_side_effects=True, vmem_limit_bytes=60 * 1024 * 1024
        ),
        name="exchange",
    )(amp, wraw, vint, virt_e, virt_l.reshape(1, -1))


def update_kernel(
    coupled, pair, lad, table, occ_e, occ_l, slab_i, slab_j, out,
    coupled_v, pair_v, out_v, lad_v, table_v, coupled_sem, pair_sem, out_sem, lad_sem, table_sem,
):
    p = lax.axis_index("wide")
    n_i, n_j, rows, n_b = pair.shape

    def loads(i):
        return (
            pltpu.make_async_copy(coupled.at[i], coupled_v.at[i], coupled_sem.at[i]),
            pltpu.make_async_copy(pair.at[i], pair_v.at[i], pair_sem.at[i]),
        )

    def store(i):
        return pltpu.make_async_copy(out_v.at[i], out.at[i], out_sem.at[i])

    load_table = pltpu.make_async_copy(table, table_v, table_sem)
    load_lad = pltpu.make_async_copy(lad, lad_v, lad_sem)
    load_table.start()
    for i in range(n_i):
        for load in loads(i):
            load.start()

    @pl.when(p == 0)
    def _():
        load_lad.start()
        load_lad.wait()

    load_table.wait()

    def step(i, carry):
        for load in loads(i):
            load.wait()
        energy_i = occ_e[slab_i[i]]
        label_i = occ_l[slab_i[i]]
        for j in range(n_j):
            energy = energy_i + occ_e[slab_j[j]]
            odd = ((label_i + occ_l[slab_j[j]]) & 1).astype(F32)

            def update(value, count):
                residual = pair_v[i, j, 0:count].astype(F32) + value
                allowed = (1.0 - odd) + (2.0 * odd - 1.0) * table_v[1, 0:count]
                return (allowed * residual / (table_v[0, 0:count] - energy)).astype(BF16)

            out_v[i, j] = update(coupled_v[i, j].astype(F32), rows)

            @pl.when(p == 0)
            def _():
                term = jnp.concatenate(
                    [lad_v[a, pl.ds(i * n_j + j, 1), :] for a in range(4)] + [jnp.zeros((12, n_b), F32)], axis=0
                )
                value = (coupled_v[i, j, 0:16].astype(F32) + term).astype(BF16).astype(F32)
                out_v[i, j, 0:16] = update(value, 16)

        store(i).start()
        return carry

    lax.fori_loop(0, n_i, step, 0)
    for i in range(n_i):
        store(i).wait()


def denominator_update(coupled, pair, lad, table, occ_e, occ_l, slab_i, slab_j):
    n_i = pair.shape[0]
    dma = pltpu.SemaphoreType.DMA
    anywhere = pl.BlockSpec(memory_space=pl.ANY)
    scalars = pl.BlockSpec(memory_space=pltpu.SMEM)
    return pl.pallas_call(
        update_kernel,
        out_shape=jax.ShapeDtypeStruct(pair.shape, BF16),
        in_specs=[anywhere] * 4 + [scalars] * 4,
        out_specs=anywhere,
        scratch_shapes=[pltpu.VMEM(pair.shape, BF16)] * 3
        + [pltpu.VMEM(lad.shape, F32), pltpu.VMEM(table.shape, F32)]
        + [dma((n_i,))] * 3
        + [dma, dma],
        compiler_params=pltpu.CompilerParams(vmem_limit_bytes=60 * 1024 * 1024),
        name="update",
    )(coupled, pair, lad, table, occ_e, occ_l, slab_i, slab_j)


def per_device(
    amplitudes,
    pair_integrals,
    cycle_integrals,
    ladder_integrals,
    occ_energy,
    virt_energy,
    occ_irrep,
    virt_irrep,
    slab_i,
    slab_j,
):
    coupled, lad, table = exchange(amplitudes, cycle_integrals, ladder_integrals, virt_energy, virt_irrep)
    return denominator_update(coupled, pair_integrals, lad, table, occ_energy, occ_irrep, slab_i, slab_j)


def solution(mesh):
    return jax.shard_map(
        per_device,
        mesh=mesh,
        in_specs=(
            P("narrow", None, "wide", None),
            P("narrow", None, "wide", None),
            P(None, None, None, "narrow"),
            P(None, None, "wide", "narrow"),
            P(),
            P(),
            P(),
            P(),
            P("narrow"),
            P(),
        ),
        out_specs=P("narrow", None, "wide", None),
        check_vma=False,
    )
```

```python
import jax
import jax.numpy as jnp
from jax import lax
from jax.experimental import pallas as pl
from jax.experimental.pallas import tpu as pltpu
from jax.sharding import PartitionSpec as P

MESH = pl.DeviceIdType.MESH
BF16 = jnp.bfloat16
F32 = jnp.float32
VBLK = 16
SIDE = 4
CHIPS = SIDE * SIDE
PLANE = 2 * CHIPS
GROUP = 16
PARTS = 6
STRAIGHT = ((1, 0), (3, 0), (0, 1), (0, 3), (2, 0), (0, 2))
TURNED = tuple((dx, dy) for dx in (1, 3, 2) for dy in (1, 3, 2))
WAYS = (0, 1)


def remote(src, dst, send_sem, recv_sem, device):
    return pltpu.make_async_remote_copy(
        src_ref=src, dst_ref=dst, send_sem=send_sem, recv_sem=recv_sem, device_id=device, device_id_type=MESH
    )


def await_bytes(ref, sem):
    pltpu.make_async_copy(ref, ref, sem).wait()


def exchange_kernel(
    amp, wraw, vint, virt_e, virt_l, coupled, lad_out, table_out,
    wraw_v, v_v, head_v, wt, a_all, prod, a_relay, c_relay, tile_out, tile_in, part, part_in, sum_v, fin_in, lad_v, table,
    load_sem, s1, s2, r1, rs, rr, sf, rf, wsend, wrecv, wfsend, wfrecv, csend, cpsend, crecv, crs, crr,
    tz_send, tz_recv, tb_send, tb_recv, tf_send, p_send, p_recv, f_send, f_recv,
):
    p = lax.axis_index("wide")
    z = lax.axis_index("narrow")
    core = lax.rem(p, 2)
    chip = lax.div(p, 2)
    x = lax.rem(chip, SIDE)
    y = lax.div(chip, SIDE)
    partner = (p + 1 - 2 * core, z)
    z_up = lax.rem(z + 1, SIDE)
    z_down = lax.rem(z + SIDE - 1, SIDE)
    z_far = lax.rem(z + 2, SIDE)
    neighbour = ((p, z_up), (p, z_down))
    z_source = (z_down, z_up)
    n_i, n_k, rows, n_b = amp.shape
    per_i = n_i // SIDE
    per_b = n_b // SIDE
    n_c = rows * PLANE
    depth = n_k * n_c
    pairs = n_i * n_k

    def place(offset):
        return lax.rem(x + offset[0] + SIDE, SIDE), lax.rem(y + offset[1] + SIDE, SIDE)

    def chip_at(offset):
        at_x, at_y = place(offset)
        return at_y * SIDE + at_x

    def back(offset):
        return (-offset[0], -offset[1])

    def via(dest, way):
        return (dest[0], 0) if way == 0 else (0, dest[1])

    def rest(dest, way):
        return (0, dest[1]) if way == 0 else (dest[0], 0)

    load_w = pltpu.make_async_copy(wraw, wraw_v, load_sem.at[0])
    load_v = pltpu.make_async_copy(vint, v_v, load_sem.at[1])
    load_h = pltpu.make_async_copy(amp.at[:, :, pl.ds(0, 16), :], head_v, load_sem.at[2])
    load_w.start()
    load_v.start()

    @pl.when(p == 0)
    def _():
        load_h.start()

    barrier = pltpu.get_barrier_semaphore()

    def greet(step, carry):
        pl.semaphore_signal(barrier, inc=1, device_id=(lax.rem(p + step, PLANE), z), device_id_type=MESH)
        return carry

    lax.fori_loop(1, PLANE, greet, 0)

    def greet_z(step, carry):
        pl.semaphore_signal(barrier, inc=1, device_id=(p, lax.rem(z + step, SIDE)), device_id_type=MESH)
        return carry

    lax.fori_loop(1, SIDE, greet_z, 0)

    load_w.wait()
    r = lax.broadcasted_iota(jnp.int32, (256, 128), 0)
    c = lax.broadcasted_iota(jnp.int32, (256, 128), 1)
    pick = jnp.where(r == 2 * c + core, 1.0, 0.0).astype(BF16)
    groups = 128 // GROUP

    def owner_of(n):
        first, owner = n * GROUP % rows // GROUP, n * GROUP // rows
        return 2 * first + owner % 2, owner // 2

    def prep(lane):
        for k in range(n_k):

            def turn(block, carry):
                at = pl.multiple_of(block * 128, 128)
                both = wraw_v[k, pl.ds(at, 128), :, lane * 128 : (lane + 1) * 128].reshape(256, 128)
                turned = lax.dot_general(both, pick, (((0,), (0,)), ((), ())), preferred_element_type=F32)
                turned = turned.astype(BF16)
                for n in range(groups):
                    g, owner_x = owner_of(lane * groups + n)
                    wt[z, g, owner_x, :, pl.ds(pl.multiple_of(k * n_c + at, 128), 128)] = turned[
                        n * GROUP : (n + 1) * GROUP
                    ]
                return carry

            lax.fori_loop(0, n_c // 128, turn, 0, unroll=4)

    def w_copy(ref, g, way):
        return remote(ref, ref, wsend.at[way, g], wrecv.at[way, g], neighbour[way])

    def w_early(lane):
        for n in range(lane * groups, (lane + 1) * groups):
            g, owner_x = owner_of(n)
            if g < 2:
                for way in range(2):
                    w_copy(wt.at[z, g, owner_x], g, way).start()

    prep(0)
    pl.semaphore_wait(barrier, PLANE - 1 + SIDE - 1)
    w_early(0)

    def a_rows(source_chip, source_core):
        return pl.ds(pl.multiple_of((2 * source_chip + source_core) * rows, rows), rows)

    def a_lanes(i):
        return pl.ds(i * per_b, per_b)

    def a_columns(at_x):
        return pl.ds(pl.multiple_of(at_x * per_b, per_b), per_b)

    def a_slot(n, way):
        return 2 * n + way

    for n, dest in enumerate(TURNED):
        at_x, at_y = place(dest)
        for way in WAYS:
            slot = a_slot(n, way)
            remote(
                amp.at[pl.ds(at_y * per_i, per_i), way, :, a_columns(at_x)], a_relay.at[slot], s1.at[slot], rr.at[slot],
                (2 * chip_at(via(dest, way)) + core, z),
            ).start()
    for n, dest in enumerate(STRAIGHT):
        at_x, at_y = place(dest)
        for i in range(per_i):
            remote(
                amp.at[at_y * per_i + i, :, :, a_columns(at_x)], a_all.at[:, a_rows(chip, core), a_lanes(i)],
                s2.at[n], r1.at[chip], (2 * chip_at(dest) + core, z),
            ).start()
    for i in range(per_i):
        pltpu.make_async_copy(
            amp.at[y * per_i + i, :, :, a_columns(x)], a_all.at[:, a_rows(chip, core), a_lanes(i)], r1.at[chip]
        ).start()

    @pl.when(p == 0)
    def _():
        load_h.wait()
        flat = head_v[...].reshape(pairs * 16, n_b)
        r = lax.broadcasted_iota(jnp.int32, (4 * 32, pairs * 16), 0)
        c = lax.broadcasted_iota(jnp.int32, (4 * 32, pairs * 16), 1)
        pair, t = r & 31, r >> 5
        pick_row = jnp.where((c == 16 * pair + t) & (pair < pairs), 1.0, 0.0).astype(BF16)
        every = jnp.dot(pick_row, flat, preferred_element_type=F32).astype(BF16)
        for t in range(4):
            for zz in range(SIDE):
                tile_out[zz, t] = every[32 * t : 32 * t + pairs, zz * per_b : (zz + 1) * per_b]
        pltpu.make_async_copy(tile_out.at[z], tile_in.at[z], tz_recv.at[z]).start()

        def send_t(step, carry):
            zz = lax.rem(z + step, SIDE)
            remote(tile_out.at[zz], tile_in.at[z], tz_send.at[zz], tz_recv.at[z], (p, zz)).start()
            return carry

        lax.fori_loop(1, SIDE, send_t, 0)

    for lane in range(1, per_b // 128):
        prep(lane)
        w_early(lane)

    def w_start(g):
        for way in range(2):
            w_copy(wt.at[z, g], g, way).start()

    def w_half(source, g, way):
        return wt.at[source, g, pl.ds(2 * way, 2)]

    def w_pass(g):
        for way in range(2):
            await_bytes(wt.at[z_source[way], g], wrecv.at[way, g])
            ref = w_half(z_source[way], g, way)
            remote(ref, ref, wfsend.at[way, g], wfrecv.at[way, g], neighbour[way]).start()

    def w_far(g):
        for way in range(2):
            await_bytes(w_half(z_far, g, way), wfrecv.at[way, g])

    for n, dest in enumerate(TURNED):
        for way in WAYS:
            slot = a_slot(n, way)
            await_bytes(a_relay.at[slot], rr.at[slot])
            source = chip_at(back(via(dest, way)))
            for i in range(per_i):
                remote(
                    a_relay.at[slot, i], a_all.at[way, a_rows(source, core), a_lanes(i)], rs.at[slot], r1.at[source],
                    (2 * chip_at(rest(dest, way)) + core, z),
                ).start()

    def pass_a(offsets):
        for offset in offsets:
            source = chip_at(back(offset))
            ref = a_all.at[:, a_rows(source, core), :]
            await_bytes(ref, r1.at[source])
            remote(ref, ref, sf.at[source], rf.at[source], partner).start()

    def tile_down():
        for dy in range(1, SIDE):
            remote(tile_in, tile_in, tb_send.at[dy + 2], tb_recv, (2 * (dy * SIDE + x), z)).start()
        remote(tile_in, tile_in, tf_send, tb_recv, partner).start()

    @pl.when(p == 0)
    def _():
        for zz in range(SIDE):
            await_bytes(tile_in.at[zz], tz_recv.at[zz])
        for dx in range(1, SIDE):
            remote(tile_in, tile_in, tb_send.at[dx - 1], tb_recv, (2 * dx, z)).start()
        tile_down()

    w_pass(0)
    w_start(2)
    w_pass(1)
    w_start(3)

    @pl.when((y == 0) & (core == 0) & (x != 0))
    def _():
        await_bytes(tile_in, tb_recv)
        tile_down()

    pass_a(((0, 0),) + STRAIGHT)

    @pl.when((y != 0) & (core == 0))
    def _():
        await_bytes(tile_in, tb_recv)
        remote(tile_in, tile_in, tf_send, tb_recv, partner).start()

    row = lax.broadcasted_iota(jnp.int32, (rows, n_b), 0)
    col = lax.broadcasted_iota(jnp.int32, (rows, n_b), 1)
    mine = col == row + p * rows
    energy = jnp.broadcast_to(virt_e[...].reshape(1, n_b), (rows, n_b))
    table[0] = energy + jnp.sum(jnp.where(mine, energy, 0.0), axis=1, keepdims=True)
    blocks = virt_l.shape[1]
    first = lax.broadcasted_iota(jnp.int32, (blocks, n_b), 0) * VBLK
    at = lax.broadcasted_iota(jnp.int32, (blocks, n_b), 1)
    member = jnp.where((at >= first) & (at < first + VBLK), 1.0, 0.0).astype(BF16)
    labels = jnp.broadcast_to((virt_l[...] & 1).astype(F32).astype(BF16), (8, blocks))
    label = jnp.dot(labels, member, preferred_element_type=F32)
    label = jnp.broadcast_to(label[0:1], (rows, n_b))
    table[1] = jnp.abs(label - jnp.sum(jnp.where(mine, label, 0.0), axis=1, keepdims=True))
    pltpu.make_async_copy(table, table_out, load_sem.at[0]).start()

    w_pass(2)
    w_start(4)

    @pl.when(core == 1)
    def _():
        await_bytes(tile_in, tb_recv)

    load_v.wait()
    for zz in range(SIDE):
        total = None
        for t in range(4):
            right = v_v[:, t].reshape(4 * rows, per_b)
            term = lax.dot_general(
                tile_in[zz, t], right, (((1,), (1,)), ((), ())), preferred_element_type=F32
            )
            total = term if total is None else total + term
        part[zz] = total
    pltpu.make_async_copy(part.at[z], part_in.at[z], p_recv.at[z]).start()

    def send_p(step, carry):
        zz = lax.rem(z + step, SIDE)
        remote(part.at[zz], part_in.at[z], p_send.at[zz], p_recv.at[z], (p, zz)).start()
        return carry

    lax.fori_loop(1, SIDE, send_p, 0)
    pass_a(TURNED)

    for zz in range(SIDE):
        await_bytes(part_in.at[zz], p_recv.at[zz])
    sum_v[...] = part_in[0] + part_in[1] + part_in[2] + part_in[3]

    @pl.when(p == 0)
    def _():
        pltpu.make_async_copy(sum_v, fin_in.at[0], f_recv).start()

    @pl.when(p != 0)
    def _():
        remote(sum_v, fin_in.at[p], f_send, f_recv, (0, z)).start()

    def got_a(source, carry):
        await_bytes(a_all.at[:, a_rows(source, 1 - core), :], rf.at[source])
        return carry

    lax.fori_loop(0, CHIPS, got_a, 0)

    def target(at_x, at_y, t, first=0, count=3):
        return coupled.at[
            pl.ds(at_y * per_i + first, count), core, pl.ds(t * GROUP, GROUP),
            pl.ds(pl.multiple_of(at_x * per_b, per_b), per_b),
        ]

    def share(g, way):
        first = 1 + g % 2
        return (0, first) if way == 0 else (first, per_i - first)

    def send_turned(g, way):
        first, count = share(g, way)
        for n, dest in enumerate(TURNED):
            remote(
                prod.at[g, chip_at(dest), pl.ds(first, count)], c_relay.at[g, n, pl.ds(first, count)],
                csend.at[g], crr.at[g, n, way], (2 * chip_at(via(dest, way)) + core, z),
            ).start()

    def send_straight(g):
        t = g // 2
        here = target(x, y, t)
        for dest in STRAIGHT:
            remote(prod.at[g, chip_at(dest)], here, csend.at[g], crecv, (2 * chip_at(dest) + g % 2, z)).start()
        if g % 2 == 1:
            remote(prod.at[2 * t + 1 - core, chip], here, cpsend.at[t], crecv, partner).start()
            pltpu.make_async_copy(prod.at[2 * t + core, chip], here, crecv).start()

    def product(g):
        left = wt[:, g].reshape(CHIPS * GROUP, depth)

        def columns(start, size):
            right = a_all[:, :, start : start + size].reshape(depth, size)
            value = jnp.dot(left, right, preferred_element_type=F32).astype(BF16)
            for lane in range(0, size, 128):
                i, at = (start + lane) // per_b, (start + lane) % per_b
                prod[g, :, i, :, at : at + 128] = value[:, lane : lane + 128].reshape(CHIPS, GROUP, 128)

        if g == PARTS - 1:
            cut = (1 + g % 2) * per_b
            columns(0, cut)
            send_turned(g, 0)
            columns(cut, per_i * per_b - cut)
            send_turned(g, 1)
        else:
            columns(0, per_i * per_b)
            send_turned(g, 0)
            send_turned(g, 1)
        send_straight(g)

    def pass_c(g):
        for n, dest in enumerate(TURNED):
            for way in WAYS:
                first, count = share(g, way)
                ref = c_relay.at[g, n, pl.ds(first, count)]
                await_bytes(ref, crr.at[g, n, way])
                at_x, at_y = place(back(via(dest, way)))
                owner = 2 * chip_at(rest(dest, way)) + g % 2
                remote(ref, target(at_x, at_y, g // 2, first, count), crs.at[g], crecv, (owner, z)).start()

    w_far(0)
    product(0)
    w_far(1)
    product(1)
    w_pass(3)
    w_start(5)
    pass_c(0)
    pass_c(1)

    @pl.when(p == 0)
    def _():
        await_bytes(fin_in, f_recv)
        for q in range(PLANE):
            for a in range(4):
                lad_v[a, :, q * rows : (q + 1) * rows] = fin_in[q, :, a * rows : (a + 1) * rows]
        pltpu.make_async_copy(lad_v, lad_out, load_sem.at[2]).start()

    w_far(2)
    product(2)
    w_pass(4)
    pass_c(2)
    w_far(3)
    product(3)
    w_pass(5)
    pass_c(3)
    w_far(4)
    product(4)
    w_far(5)
    product(5)
    pass_c(4)
    pass_c(5)

    for slot in range(2 * len(TURNED)):
        await_bytes(a_relay.at[slot], s1.at[slot])
        await_bytes(a_relay.at[slot], rs.at[slot])
    for n in range(len(STRAIGHT)):
        await_bytes(a_all.at[:, pl.ds(0, rows), :], s2.at[n])

    def passed_a(step, carry):
        await_bytes(a_all.at[:, a_rows(step, core), :], sf.at[step])
        return carry

    lax.fori_loop(0, CHIPS, passed_a, 0)
    for way in range(2):
        for g in range(PARTS):
            await_bytes(wt.at[z, g], wsend.at[way, g])
            await_bytes(w_half(z, g, way), wfsend.at[way, g])

    def sent_p(step, carry):
        zz = lax.rem(z + step, SIDE)
        await_bytes(part.at[zz], p_send.at[zz])
        return carry

    lax.fori_loop(1, SIDE, sent_p, 0)

    @pl.when(core == 0)
    def _():
        await_bytes(tile_in, tf_send)

    @pl.when((y == 0) & (core == 0))
    def _():
        for dy in range(1, SIDE):
            await_bytes(tile_in, tb_send.at[dy + 2])

    @pl.when(p == 0)
    def _():
        def sent_t(step, carry):
            zz = lax.rem(z + step, SIDE)
            await_bytes(tile_out.at[zz], tz_send.at[zz])
            return carry

        lax.fori_loop(1, SIDE, sent_t, 0)
        for dx in range(1, SIDE):
            await_bytes(tile_in, tb_send.at[dx - 1])
        await_bytes(lad_v, load_sem.at[2])

    @pl.when(p != 0)
    def _():
        await_bytes(sum_v, f_send)

    await_bytes(table, load_sem.at[0])
    for g in range(PARTS):
        await_bytes(prod.at[g, pl.ds(0, CHIPS - 1)], csend.at[g])
        await_bytes(c_relay.at[g], crs.at[g])
    for t in range(PARTS // 2):
        await_bytes(prod.at[t, 0], cpsend.at[t])
    await_bytes(coupled, crecv)


def exchange(amp, wraw, vint, virt_e, virt_l):
    n_i, n_k, rows, n_b = amp.shape
    per_i, per_b, n_c = n_i // SIDE, n_b // SIDE, rows * PLANE
    pairs, turned = n_i * n_k, len(TURNED)
    dma = pltpu.SemaphoreType.DMA
    anywhere = pl.BlockSpec(memory_space=pl.ANY)
    inside = pl.BlockSpec(memory_space=pltpu.VMEM)
    return pl.pallas_call(
        exchange_kernel,
        out_shape=(
            jax.ShapeDtypeStruct(amp.shape, BF16),
            jax.ShapeDtypeStruct((4, pairs, n_b), F32),
            jax.ShapeDtypeStruct((2, rows, n_b), F32),
        ),
        in_specs=[anywhere] * 3 + [inside] * 2,
        out_specs=(anywhere,) * 3,
        scratch_shapes=[
            pltpu.VMEM(wraw.shape, BF16),
            pltpu.VMEM(vint.shape, BF16),
            pltpu.VMEM((n_i, n_k, 16, n_b), BF16),
            pltpu.VMEM((SIDE, PARTS, SIDE, GROUP, n_k * n_c), BF16),
            pltpu.VMEM((n_k, n_c, per_i * per_b), BF16),
            pltpu.VMEM((PARTS, CHIPS, per_i, GROUP, per_b), BF16),
            pltpu.VMEM((2 * turned, per_i, rows, per_b), BF16),
            pltpu.VMEM((PARTS, turned, per_i, GROUP, per_b), BF16),
            pltpu.VMEM((SIDE, 4, pairs, per_b), BF16),
            pltpu.VMEM((SIDE, 4, pairs, per_b), BF16),
            pltpu.VMEM((SIDE, pairs, 4 * rows), F32),
            pltpu.VMEM((SIDE, pairs, 4 * rows), F32),
            pltpu.VMEM((pairs, 4 * rows), F32),
            pltpu.VMEM((PLANE, pairs, 4 * rows), F32),
            pltpu.VMEM((4, pairs, n_b), F32),
            pltpu.VMEM((2, rows, n_b), F32),
            dma((3,)),
            dma((2 * turned,)),
            dma((len(STRAIGHT),)),
            dma((CHIPS,)),
            dma((2 * turned,)),
            dma((2 * turned,)),
            dma((CHIPS,)),
            dma((CHIPS,)),
            dma((2, PARTS)),
            dma((2, PARTS)),
            dma((2, PARTS)),
            dma((2, PARTS)),
            dma((PARTS,)),
            dma((PARTS // 2,)),
            dma,
            dma((PARTS,)),
            dma((PARTS, turned, 2)),
            dma((SIDE,)),
            dma((SIDE,)),
            dma((6,)),
            dma,
            dma,
            dma((SIDE,)),
            dma((SIDE,)),
            dma,
            dma,
        ],
        compiler_params=pltpu.CompilerParams(
            collective_id=0, has_side_effects=True, vmem_limit_bytes=60 * 1024 * 1024
        ),
        name="exchange",
    )(amp, wraw, vint, virt_e, virt_l.reshape(1, -1))


def update_kernel(
    coupled, pair, lad, table, occ_e, occ_l, slab_i, slab_j, out,
    coupled_v, pair_v, out_v, lad_v, table_v, coupled_sem, pair_sem, out_sem, lad_sem, table_sem,
):
    p = lax.axis_index("wide")
    n_i, n_j, rows, n_b = pair.shape

    def loads(i):
        return (
            pltpu.make_async_copy(coupled.at[i], coupled_v.at[i], coupled_sem.at[i]),
            pltpu.make_async_copy(pair.at[i], pair_v.at[i], pair_sem.at[i]),
        )

    def store(i):
        return pltpu.make_async_copy(out_v.at[i], out.at[i], out_sem.at[i])

    load_table = pltpu.make_async_copy(table, table_v, table_sem)
    load_lad = pltpu.make_async_copy(lad, lad_v, lad_sem)
    load_table.start()
    for i in range(n_i):
        for load in loads(i):
            load.start()

    @pl.when(p == 0)
    def _():
        load_lad.start()
        load_lad.wait()

    load_table.wait()

    def step(i, carry):
        for load in loads(i):
            load.wait()
        energy_i = occ_e[slab_i[i]]
        label_i = occ_l[slab_i[i]]
        for j in range(n_j):
            energy = energy_i + occ_e[slab_j[j]]
            odd = ((label_i + occ_l[slab_j[j]]) & 1).astype(F32)

            def update(value, count):
                residual = pair_v[i, j, 0:count].astype(F32) + value
                allowed = (1.0 - odd) + (2.0 * odd - 1.0) * table_v[1, 0:count]
                return (allowed * residual / (table_v[0, 0:count] - energy)).astype(BF16)

            out_v[i, j] = update(coupled_v[i, j].astype(F32), rows)

            @pl.when(p == 0)
            def _():
                term = jnp.concatenate(
                    [lad_v[a, pl.ds(i * n_j + j, 1), :] for a in range(4)] + [jnp.zeros((12, n_b), F32)], axis=0
                )
                value = (coupled_v[i, j, 0:16].astype(F32) + term).astype(BF16).astype(F32)
                out_v[i, j, 0:16] = update(value, 16)

        store(i).start()
        return carry

    lax.fori_loop(0, n_i, step, 0)
    for i in range(n_i):
        store(i).wait()


def denominator_update(coupled, pair, lad, table, occ_e, occ_l, slab_i, slab_j):
    n_i = pair.shape[0]
    dma = pltpu.SemaphoreType.DMA
    anywhere = pl.BlockSpec(memory_space=pl.ANY)
    scalars = pl.BlockSpec(memory_space=pltpu.SMEM)
    return pl.pallas_call(
        update_kernel,
        out_shape=jax.ShapeDtypeStruct(pair.shape, BF16),
        in_specs=[anywhere] * 4 + [scalars] * 4,
        out_specs=anywhere,
        scratch_shapes=[pltpu.VMEM(pair.shape, BF16)] * 3
        + [pltpu.VMEM(lad.shape, F32), pltpu.VMEM(table.shape, F32)]
        + [dma((n_i,))] * 3
        + [dma, dma],
        compiler_params=pltpu.CompilerParams(vmem_limit_bytes=60 * 1024 * 1024),
        name="update",
    )(coupled, pair, lad, table, occ_e, occ_l, slab_i, slab_j)


def per_device(
    amplitudes,
    pair_integrals,
    cycle_integrals,
    ladder_integrals,
    occ_energy,
    virt_energy,
    occ_irrep,
    virt_irrep,
    slab_i,
    slab_j,
):
    coupled, lad, table = exchange(amplitudes, cycle_integrals, ladder_integrals, virt_energy, virt_irrep)
    return denominator_update(coupled, pair_integrals, lad, table, occ_energy, occ_irrep, slab_i, slab_j)


def solution(mesh):
    return jax.shard_map(
        per_device,
        mesh=mesh,
        in_specs=(
            P("narrow", None, "wide", None),
            P("narrow", None, "wide", None),
            P(None, None, None, "narrow"),
            P(None, None, "wide", "narrow"),
            P(),
            P(),
            P(),
            P(),
            P("narrow"),
            P(),
        ),
        out_specs=P("narrow", None, "wide", None),
        check_vma=False,
    )
```

```python
import jax
import jax.numpy as jnp
from jax import lax
from jax.experimental import pallas as pl
from jax.experimental.pallas import tpu as pltpu
from jax.sharding import PartitionSpec as P

MESH = pl.DeviceIdType.MESH
BF16 = jnp.bfloat16
F32 = jnp.float32
VBLK = 16
SIDE = 4
CHIPS = SIDE * SIDE
PLANE = 2 * CHIPS
GROUP = 16
PARTS = 6
STRAIGHT = ((1, 0), (3, 0), (0, 1), (0, 3), (2, 0), (0, 2))
TURNED = tuple((dx, dy) for dx in (1, 3, 2) for dy in (1, 3, 2))
WAYS = (0, 1)


def remote(src, dst, send_sem, recv_sem, device):
    return pltpu.make_async_remote_copy(
        src_ref=src, dst_ref=dst, send_sem=send_sem, recv_sem=recv_sem, device_id=device, device_id_type=MESH
    )


def await_bytes(ref, sem):
    pltpu.make_async_copy(ref, ref, sem).wait()


def exchange_kernel(
    amp, wraw, vint, virt_e, virt_l, coupled, lad_out, table_out,
    wraw_v, v_v, head_v, wt, a_all, prod, a_relay, c_relay, tile_out, tile_in, part, part_in, sum_v, fin_in, lad_v, table,
    load_sem, s1, s2, r1, rs, rr, sf, rf, wsend, wrecv, wfsend, wfrecv, csend, cpsend, crecv, crs, crr,
    tz_send, tz_recv, tb_send, tb_recv, tf_send, p_send, p_recv, f_send, f_recv,
):
    p = lax.axis_index("wide")
    z = lax.axis_index("narrow")
    core = lax.rem(p, 2)
    chip = lax.div(p, 2)
    x = lax.rem(chip, SIDE)
    y = lax.div(chip, SIDE)
    partner = (p + 1 - 2 * core, z)
    z_up = lax.rem(z + 1, SIDE)
    z_down = lax.rem(z + SIDE - 1, SIDE)
    z_far = lax.rem(z + 2, SIDE)
    neighbour = ((p, z_up), (p, z_down))
    z_source = (z_down, z_up)
    n_i, n_k, rows, n_b = amp.shape
    per_i = n_i // SIDE
    per_b = n_b // SIDE
    n_c = rows * PLANE
    depth = n_k * n_c
    pairs = n_i * n_k

    def place(offset):
        return lax.rem(x + offset[0] + SIDE, SIDE), lax.rem(y + offset[1] + SIDE, SIDE)

    def chip_at(offset):
        at_x, at_y = place(offset)
        return at_y * SIDE + at_x

    def back(offset):
        return (-offset[0], -offset[1])

    def via(dest, way):
        return (dest[0], 0) if way == 0 else (0, dest[1])

    def rest(dest, way):
        return (0, dest[1]) if way == 0 else (dest[0], 0)

    load_w = [pltpu.make_async_copy(wraw.at[k], wraw_v.at[k], load_sem.at[3 * k]) for k in range(n_k)]
    load_v = pltpu.make_async_copy(vint, v_v, load_sem.at[1])
    load_h = pltpu.make_async_copy(amp.at[:, :, pl.ds(0, 16), :], head_v, load_sem.at[2])
    for load in load_w:
        load.start()
    load_v.start()

    @pl.when(p == 0)
    def _():
        load_h.start()

    barrier = pltpu.get_barrier_semaphore()

    def greet(step, carry):
        pl.semaphore_signal(barrier, inc=1, device_id=(lax.rem(p + step, PLANE), z), device_id_type=MESH)
        return carry

    lax.fori_loop(1, PLANE, greet, 0)

    def greet_z(step, carry):
        pl.semaphore_signal(barrier, inc=1, device_id=(p, lax.rem(z + step, SIDE)), device_id_type=MESH)
        return carry

    lax.fori_loop(1, SIDE, greet_z, 0)

    r = lax.broadcasted_iota(jnp.int32, (256, 128), 0)
    c = lax.broadcasted_iota(jnp.int32, (256, 128), 1)
    pick = jnp.where(r == 2 * c + core, 1.0, 0.0).astype(BF16)
    groups = 128 // GROUP

    def owner_of(n):
        first, owner = n * GROUP % rows // GROUP, n * GROUP // rows
        return 2 * first + owner % 2, owner // 2

    def prep(lane):
        for k in range(n_k):
            if lane == 0:
                load_w[k].wait()

            def turn(block, carry):
                at = pl.multiple_of(block * 128, 128)
                both = wraw_v[k, pl.ds(at, 128), :, lane * 128 : (lane + 1) * 128].reshape(256, 128)
                turned = lax.dot_general(both, pick, (((0,), (0,)), ((), ())), preferred_element_type=F32)
                turned = turned.astype(BF16)
                for n in range(groups):
                    g, owner_x = owner_of(lane * groups + n)
                    wt[z, g, owner_x, :, pl.ds(pl.multiple_of(k * n_c + at, 128), 128)] = turned[
                        n * GROUP : (n + 1) * GROUP
                    ]
                return carry

            lax.fori_loop(0, n_c // 128, turn, 0, unroll=4)

    def w_copy(ref, g, way):
        return remote(ref, ref, wsend.at[way, g], wrecv.at[way, g], neighbour[way])

    def w_early(lane):
        for n in range(lane * groups, (lane + 1) * groups):
            g, owner_x = owner_of(n)
            if g < 2:
                for way in range(2):
                    w_copy(wt.at[z, g, owner_x], g, way).start()

    prep(0)
    pl.semaphore_wait(barrier, PLANE - 1 + SIDE - 1)
    w_early(0)

    def a_rows(source_chip, source_core):
        return pl.ds(pl.multiple_of((2 * source_chip + source_core) * rows, rows), rows)

    def a_lanes(i):
        return pl.ds(i * per_b, per_b)

    def a_columns(at_x):
        return pl.ds(pl.multiple_of(at_x * per_b, per_b), per_b)

    def a_slot(n, way):
        return 2 * n + way

    def send_a_turned():
        for n, dest in enumerate(TURNED):
            at_x, at_y = place(dest)
            for way in WAYS:
                slot = a_slot(n, way)
                remote(
                    amp.at[pl.ds(at_y * per_i, per_i), way, :, a_columns(at_x)], a_relay.at[slot], s1.at[slot], rr.at[slot],
                    (2 * chip_at(via(dest, way)) + core, z),
                ).start()

    def send_a_straight():
        for n, dest in enumerate(STRAIGHT):
            at_x, at_y = place(dest)
            for i in range(per_i):
                remote(
                    amp.at[at_y * per_i + i, :, :, a_columns(at_x)], a_all.at[:, a_rows(chip, core), a_lanes(i)],
                    s2.at[n], r1.at[chip], (2 * chip_at(dest) + core, z),
                ).start()
        for i in range(per_i):
            pltpu.make_async_copy(
                amp.at[y * per_i + i, :, :, a_columns(x)], a_all.at[:, a_rows(chip, core), a_lanes(i)], r1.at[chip]
            ).start()

    def tile_down():
        for dy in range(1, SIDE):
            remote(tile_in, tile_in, tb_send.at[dy + 2], tb_recv, (2 * (dy * SIDE + x), z)).start()
        remote(tile_in, tile_in, tf_send, tb_recv, partner).start()

    @pl.when(p != 0)
    def _():
        send_a_turned()

    @pl.when(p == 0)
    def _():
        load_h.wait()
        flat = head_v[...].reshape(pairs * 16, n_b)
        r = lax.broadcasted_iota(jnp.int32, (4 * pairs, pairs * 16), 0)
        c = lax.broadcasted_iota(jnp.int32, (4 * pairs, pairs * 16), 1)
        t = sum((r >= n * pairs).astype(jnp.int32) for n in range(1, 4))
        pick_row = jnp.where(c == 16 * (r - pairs * t) + t, 1.0, 0.0).astype(BF16)
        every = jnp.dot(pick_row, flat, preferred_element_type=F32).astype(BF16)
        for zz in range(SIDE):
            tile_out[zz] = every[:, zz * per_b : (zz + 1) * per_b]
        pltpu.make_async_copy(tile_out.at[z], tile_in.at[z], tz_recv.at[z]).start()

        def send_t(step, carry):
            zz = lax.rem(z + step, SIDE)
            remote(tile_out.at[zz], tile_in.at[z], tz_send.at[zz], tz_recv.at[z], (p, zz)).start()
            return carry

        lax.fori_loop(1, SIDE, send_t, 0)

    prep(1)
    w_early(1)

    @pl.when(p == 0)
    def _():
        for zz in range(SIDE):
            await_bytes(tile_in.at[zz], tz_recv.at[zz])
        for dx in range(1, SIDE):
            remote(tile_in, tile_in, tb_send.at[dx - 1], tb_recv, (2 * dx, z)).start()
        tile_down()
        send_a_turned()

    prep(2)
    w_early(2)

    @pl.when((y == 0) & (core == 0) & (x != 0))
    def _():
        await_bytes(tile_in, tb_recv)
        tile_down()

    send_a_straight()

    def w_start(g):
        for way in range(2):
            w_copy(wt.at[z, g], g, way).start()

    def w_half(source, g, way):
        return wt.at[source, g, pl.ds(2 * way, 2)]

    def w_pass(g):
        for way in range(2):
            await_bytes(wt.at[z_source[way], g], wrecv.at[way, g])
            ref = w_half(z_source[way], g, way)
            remote(ref, ref, wfsend.at[way, g], wfrecv.at[way, g], neighbour[way]).start()

    def w_far(g):
        for way in range(2):
            await_bytes(w_half(z_far, g, way), wfrecv.at[way, g])

    def pass_a(offsets):
        for offset in offsets:
            source = chip_at(back(offset))
            ref = a_all.at[:, a_rows(source, core), :]
            await_bytes(ref, r1.at[source])
            remote(ref, ref, sf.at[source], rf.at[source], partner).start()

    w_pass(0)
    w_start(2)

    for n, dest in enumerate(TURNED):
        for way in WAYS:
            slot = a_slot(n, way)
            await_bytes(a_relay.at[slot], rr.at[slot])
            source = chip_at(back(via(dest, way)))
            for i in range(per_i):
                remote(
                    a_relay.at[slot, i], a_all.at[way, a_rows(source, core), a_lanes(i)], rs.at[slot], r1.at[source],
                    (2 * chip_at(rest(dest, way)) + core, z),
                ).start()

    w_pass(1)
    w_start(3)

    @pl.when((y != 0) & (core == 0))
    def _():
        await_bytes(tile_in, tb_recv)
        remote(tile_in, tile_in, tf_send, tb_recv, partner).start()

    pass_a(((0, 0),) + STRAIGHT)

    row = lax.broadcasted_iota(jnp.int32, (rows, n_b), 0)
    col = lax.broadcasted_iota(jnp.int32, (rows, n_b), 1)
    mine = col == row + p * rows
    energy = jnp.broadcast_to(virt_e[...].reshape(1, n_b), (rows, n_b))
    table[0] = energy + jnp.sum(jnp.where(mine, energy, 0.0), axis=1, keepdims=True)
    blocks = virt_l.shape[1]
    first = lax.broadcasted_iota(jnp.int32, (blocks, n_b), 0) * VBLK
    at = lax.broadcasted_iota(jnp.int32, (blocks, n_b), 1)
    member = jnp.where((at >= first) & (at < first + VBLK), 1.0, 0.0).astype(BF16)
    labels = jnp.broadcast_to((virt_l[...] & 1).astype(F32).astype(BF16), (8, blocks))
    label = jnp.dot(labels, member, preferred_element_type=F32)
    label = jnp.broadcast_to(label[0:1], (rows, n_b))
    table[1] = jnp.abs(label - jnp.sum(jnp.where(mine, label, 0.0), axis=1, keepdims=True))
    pltpu.make_async_copy(table, table_out, load_sem.at[0]).start()

    w_pass(2)
    w_start(4)

    @pl.when(core == 1)
    def _():
        await_bytes(tile_in, tb_recv)

    load_v.wait()
    for zz in range(SIDE):
        total = None
        for t in range(4):
            right = v_v[:, t].reshape(4 * rows, per_b)
            term = lax.dot_general(
                tile_in[zz, t * pairs : (t + 1) * pairs], right, (((1,), (1,)), ((), ())), preferred_element_type=F32
            )
            total = term if total is None else total + term
        part[zz] = total
    pltpu.make_async_copy(part.at[z], part_in.at[z], p_recv.at[z]).start()

    def send_p(step, carry):
        zz = lax.rem(z + step, SIDE)
        remote(part.at[zz], part_in.at[z], p_send.at[zz], p_recv.at[z], (p, zz)).start()
        return carry

    lax.fori_loop(1, SIDE, send_p, 0)

    pass_a(TURNED)

    def got_a(source, carry):
        await_bytes(a_all.at[:, a_rows(source, 1 - core), :], rf.at[source])
        return carry

    lax.fori_loop(0, CHIPS, got_a, 0)

    def target(at_x, at_y, t, first=0, count=3):
        return coupled.at[
            pl.ds(at_y * per_i + first, count), core, pl.ds(t * GROUP, GROUP),
            pl.ds(pl.multiple_of(at_x * per_b, per_b), per_b),
        ]

    def share(g, way):
        first = 1 + g % 2
        return (0, first) if way == 0 else (first, per_i - first)

    def send_turned(g, way):
        first, count = share(g, way)
        for n, dest in enumerate(TURNED):
            remote(
                prod.at[g, chip_at(dest), pl.ds(first, count)], c_relay.at[g, n, pl.ds(first, count)],
                csend.at[g], crr.at[g, n, way], (2 * chip_at(via(dest, way)) + core, z),
            ).start()

    def send_straight(g):
        t = g // 2
        here = target(x, y, t)
        for dest in STRAIGHT:
            remote(prod.at[g, chip_at(dest)], here, csend.at[g], crecv, (2 * chip_at(dest) + g % 2, z)).start()
        if g % 2 == 1:
            remote(prod.at[2 * t + 1 - core, chip], here, cpsend.at[t], crecv, partner).start()
            pltpu.make_async_copy(prod.at[2 * t + core, chip], here, crecv).start()

    def product(g):
        left = wt[:, g].reshape(CHIPS * GROUP, depth)

        def columns(start, size):
            right = a_all[:, :, start : start + size].reshape(depth, size)
            value = jnp.dot(left, right, preferred_element_type=F32).astype(BF16)
            for lane in range(0, size, 128):
                i, at = (start + lane) // per_b, (start + lane) % per_b
                prod[g, :, i, :, at : at + 128] = value[:, lane : lane + 128].reshape(CHIPS, GROUP, 128)

        if g == PARTS - 1:
            cut = (1 + g % 2) * per_b
            columns(0, cut)
            send_turned(g, 0)
            columns(cut, per_i * per_b - cut)
            send_turned(g, 1)
        else:
            columns(0, per_i * per_b)
            send_turned(g, 0)
            send_turned(g, 1)
        send_straight(g)

    def pass_c(g):
        for n, dest in enumerate(TURNED):
            for way in WAYS:
                first, count = share(g, way)
                ref = c_relay.at[g, n, pl.ds(first, count)]
                await_bytes(ref, crr.at[g, n, way])
                at_x, at_y = place(back(via(dest, way)))
                owner = 2 * chip_at(rest(dest, way)) + g % 2
                remote(ref, target(at_x, at_y, g // 2, first, count), crs.at[g], crecv, (owner, z)).start()

    w_far(0)
    product(0)
    w_far(1)
    product(1)
    w_pass(3)
    w_start(5)
    pass_c(0)
    pass_c(1)

    w_far(2)
    product(2)
    w_pass(4)
    pass_c(2)
    w_far(3)
    product(3)

    for zz in range(SIDE):
        await_bytes(part_in.at[zz], p_recv.at[zz])
    sum_v[...] = part_in[0] + part_in[1] + part_in[2] + part_in[3]

    @pl.when(p == 0)
    def _():
        pltpu.make_async_copy(sum_v, fin_in.at[0], f_recv).start()

    @pl.when(p != 0)
    def _():
        remote(sum_v, fin_in.at[p], f_send, f_recv, (0, z)).start()

    w_pass(5)
    pass_c(3)

    w_far(4)
    product(4)
    w_far(5)
    product(5)
    pass_c(4)
    pass_c(5)

    @pl.when(p == 0)
    def _():
        await_bytes(fin_in, f_recv)
        for q in range(PLANE):
            for a in range(4):
                lad_v[a, :, q * rows : (q + 1) * rows] = fin_in[q, :, a * rows : (a + 1) * rows]
        pltpu.make_async_copy(lad_v, lad_out, load_sem.at[2]).start()


    for slot in range(2 * len(TURNED)):
        await_bytes(a_relay.at[slot], s1.at[slot])
        await_bytes(a_relay.at[slot], rs.at[slot])
    for n in range(len(STRAIGHT)):
        await_bytes(a_all.at[:, pl.ds(0, rows), :], s2.at[n])

    def passed_a(step, carry):
        await_bytes(a_all.at[:, a_rows(step, core), :], sf.at[step])
        return carry

    lax.fori_loop(0, CHIPS, passed_a, 0)
    for way in range(2):
        for g in range(PARTS):
            await_bytes(wt.at[z, g], wsend.at[way, g])
            await_bytes(w_half(z, g, way), wfsend.at[way, g])

    def sent_p(step, carry):
        zz = lax.rem(z + step, SIDE)
        await_bytes(part.at[zz], p_send.at[zz])
        return carry

    lax.fori_loop(1, SIDE, sent_p, 0)

    @pl.when(core == 0)
    def _():
        await_bytes(tile_in, tf_send)

    @pl.when((y == 0) & (core == 0))
    def _():
        for dy in range(1, SIDE):
            await_bytes(tile_in, tb_send.at[dy + 2])

    @pl.when(p == 0)
    def _():
        def sent_t(step, carry):
            zz = lax.rem(z + step, SIDE)
            await_bytes(tile_out.at[zz], tz_send.at[zz])
            return carry

        lax.fori_loop(1, SIDE, sent_t, 0)
        for dx in range(1, SIDE):
            await_bytes(tile_in, tb_send.at[dx - 1])
        await_bytes(lad_v, load_sem.at[2])

    @pl.when(p != 0)
    def _():
        await_bytes(sum_v, f_send)

    await_bytes(table, load_sem.at[0])
    for g in range(PARTS):
        await_bytes(prod.at[g, pl.ds(0, CHIPS - 1)], csend.at[g])
        await_bytes(c_relay.at[g], crs.at[g])
    for t in range(PARTS // 2):
        await_bytes(prod.at[t, 0], cpsend.at[t])
    await_bytes(coupled, crecv)


def exchange(amp, wraw, vint, virt_e, virt_l):
    n_i, n_k, rows, n_b = amp.shape
    per_i, per_b, n_c = n_i // SIDE, n_b // SIDE, rows * PLANE
    pairs, turned = n_i * n_k, len(TURNED)
    dma = pltpu.SemaphoreType.DMA
    anywhere = pl.BlockSpec(memory_space=pl.ANY)
    inside = pl.BlockSpec(memory_space=pltpu.VMEM)
    return pl.pallas_call(
        exchange_kernel,
        out_shape=(
            jax.ShapeDtypeStruct(amp.shape, BF16),
            jax.ShapeDtypeStruct((4, pairs, n_b), F32),
            jax.ShapeDtypeStruct((2, rows, n_b), F32),
        ),
        in_specs=[anywhere] * 3 + [inside] * 2,
        out_specs=(anywhere,) * 3,
        scratch_shapes=[
            pltpu.VMEM(wraw.shape, BF16),
            pltpu.VMEM(vint.shape, BF16),
            pltpu.VMEM((n_i, n_k, 16, n_b), BF16),
            pltpu.VMEM((SIDE, PARTS, SIDE, GROUP, n_k * n_c), BF16),
            pltpu.VMEM((n_k, n_c, per_i * per_b), BF16),
            pltpu.VMEM((PARTS, CHIPS, per_i, GROUP, per_b), BF16),
            pltpu.VMEM((2 * turned, per_i, rows, per_b), BF16),
            pltpu.VMEM((PARTS, turned, per_i, GROUP, per_b), BF16),
            pltpu.VMEM((SIDE, 4 * pairs, per_b), BF16),
            pltpu.VMEM((SIDE, 4 * pairs, per_b), BF16),
            pltpu.VMEM((SIDE, pairs, 4 * rows), F32),
            pltpu.VMEM((SIDE, pairs, 4 * rows), F32),
            pltpu.VMEM((pairs, 4 * rows), F32),
            pltpu.VMEM((PLANE, pairs, 4 * rows), F32),
            pltpu.VMEM((4, pairs, n_b), F32),
            pltpu.VMEM((2, rows, n_b), F32),
            dma((4,)),
            dma((2 * turned,)),
            dma((len(STRAIGHT),)),
            dma((CHIPS,)),
            dma((2 * turned,)),
            dma((2 * turned,)),
            dma((CHIPS,)),
            dma((CHIPS,)),
            dma((2, PARTS)),
            dma((2, PARTS)),
            dma((2, PARTS)),
            dma((2, PARTS)),
            dma((PARTS,)),
            dma((PARTS // 2,)),
            dma,
            dma((PARTS,)),
            dma((PARTS, turned, 2)),
            dma((SIDE,)),
            dma((SIDE,)),
            dma((6,)),
            dma,
            dma,
            dma((SIDE,)),
            dma((SIDE,)),
            dma,
            dma,
        ],
        compiler_params=pltpu.CompilerParams(
            collective_id=0, has_side_effects=True, vmem_limit_bytes=60 * 1024 * 1024
        ),
        name="exchange",
    )(amp, wraw, vint, virt_e, virt_l.reshape(1, -1))


def update_kernel(
    coupled, pair, lad, table, occ_e, occ_l, slab_i, slab_j, out,
    coupled_v, pair_v, out_v, lad_v, table_v, coupled_sem, pair_sem, out_sem, lad_sem, table_sem,
):
    p = lax.axis_index("wide")
    n_i, n_j, rows, n_b = pair.shape

    def loads(i):
        return (
            pltpu.make_async_copy(coupled.at[i], coupled_v.at[i], coupled_sem.at[i]),
            pltpu.make_async_copy(pair.at[i], pair_v.at[i], pair_sem.at[i]),
        )

    def store(i):
        return pltpu.make_async_copy(out_v.at[i], out.at[i], out_sem.at[i])

    load_table = pltpu.make_async_copy(table, table_v, table_sem)
    load_lad = pltpu.make_async_copy(lad, lad_v, lad_sem)
    load_table.start()
    for i in range(n_i):
        for load in loads(i):
            load.start()

    @pl.when(p == 0)
    def _():
        load_lad.start()
        load_lad.wait()

    load_table.wait()

    def step(i, carry):
        for load in loads(i):
            load.wait()
        energy_i = occ_e[slab_i[i]]
        label_i = occ_l[slab_i[i]]
        for j in range(n_j):
            energy = energy_i + occ_e[slab_j[j]]
            odd = ((label_i + occ_l[slab_j[j]]) & 1).astype(F32)

            def update(value, count):
                residual = pair_v[i, j, 0:count].astype(F32) + value
                allowed = (1.0 - odd) + (2.0 * odd - 1.0) * table_v[1, 0:count]
                return (allowed * residual / (table_v[0, 0:count] - energy)).astype(BF16)

            out_v[i, j] = update(coupled_v[i, j].astype(F32), rows)

            @pl.when(p == 0)
            def _():
                term = jnp.concatenate(
                    [lad_v[a, pl.ds(i * n_j + j, 1), :] for a in range(4)] + [jnp.zeros((12, n_b), F32)], axis=0
                )
                value = (coupled_v[i, j, 0:16].astype(F32) + term).astype(BF16).astype(F32)
                out_v[i, j, 0:16] = update(value, 16)

        store(i).start()
        return carry

    lax.fori_loop(0, n_i, step, 0)
    for i in range(n_i):
        store(i).wait()


def denominator_update(coupled, pair, lad, table, occ_e, occ_l, slab_i, slab_j):
    n_i = pair.shape[0]
    dma = pltpu.SemaphoreType.DMA
    anywhere = pl.BlockSpec(memory_space=pl.ANY)
    scalars = pl.BlockSpec(memory_space=pltpu.SMEM)
    return pl.pallas_call(
        update_kernel,
        out_shape=jax.ShapeDtypeStruct(pair.shape, BF16),
        in_specs=[anywhere] * 4 + [scalars] * 4,
        out_specs=anywhere,
        scratch_shapes=[pltpu.VMEM(pair.shape, BF16)] * 3
        + [pltpu.VMEM(lad.shape, F32), pltpu.VMEM(table.shape, F32)]
        + [dma((n_i,))] * 3
        + [dma, dma],
        compiler_params=pltpu.CompilerParams(vmem_limit_bytes=60 * 1024 * 1024),
        name="update",
    )(coupled, pair, lad, table, occ_e, occ_l, slab_i, slab_j)


def per_device(
    amplitudes,
    pair_integrals,
    cycle_integrals,
    ladder_integrals,
    occ_energy,
    virt_energy,
    occ_irrep,
    virt_irrep,
    slab_i,
    slab_j,
):
    coupled, lad, table = exchange(amplitudes, cycle_integrals, ladder_integrals, virt_energy, virt_irrep)
    return denominator_update(coupled, pair_integrals, lad, table, occ_energy, occ_irrep, slab_i, slab_j)


def solution(mesh):
    return jax.shard_map(
        per_device,
        mesh=mesh,
        in_specs=(
            P("narrow", None, "wide", None),
            P("narrow", None, "wide", None),
            P(None, None, None, "narrow"),
            P(None, None, "wide", "narrow"),
            P(),
            P(),
            P(),
            P(),
            P("narrow"),
            P(),
        ),
        out_specs=P("narrow", None, "wide", None),
        check_vma=False,
    )
```

```python
import jax
import jax.numpy as jnp
from jax import lax
from jax.experimental import pallas as pl
from jax.experimental.pallas import tpu as pltpu
from jax.sharding import PartitionSpec as P

MESH = pl.DeviceIdType.MESH
BF16 = jnp.bfloat16
F32 = jnp.float32
VBLK = 16
SIDE = 4
CHIPS = SIDE * SIDE
PLANE = 2 * CHIPS
GROUP = 16
PARTS = 6
STRAIGHT = ((1, 0), (3, 0), (0, 1), (0, 3), (2, 0), (0, 2))
TURNED = tuple((dx, dy) for dx in (1, 3, 2) for dy in (1, 3, 2))
WAYS = (0, 1)


def remote(src, dst, send_sem, recv_sem, device):
    return pltpu.make_async_remote_copy(
        src_ref=src, dst_ref=dst, send_sem=send_sem, recv_sem=recv_sem, device_id=device, device_id_type=MESH
    )


def await_bytes(ref, sem):
    pltpu.make_async_copy(ref, ref, sem).wait()


def exchange_kernel(
    amp, wraw, vint, pair_in, virt_e, virt_l, occ_e, occ_l, slab_i, slab_j, out,
    coupled, pair_v, out_v,
    wraw_v, v_v, head_v, wt, a_all, prod, a_relay, c_relay, tile_out, tile_in, part, part_in, sum_v, fin_in, lad_v, table,
    load_sem, s1, s2, r1, rs, rr, sf, rf, wsend, wrecv, wfsend, wfrecv, csend, cpsend, crecv, crs, crr,
    pair_sem, out_sem, tz_send, tz_recv, tb_send, tb_recv, tf_send, p_send, p_recv, f_send, f_recv,
):
    p = lax.axis_index("wide")
    z = lax.axis_index("narrow")
    core = lax.rem(p, 2)
    chip = lax.div(p, 2)
    x = lax.rem(chip, SIDE)
    y = lax.div(chip, SIDE)
    partner = (p + 1 - 2 * core, z)
    z_up = lax.rem(z + 1, SIDE)
    z_down = lax.rem(z + SIDE - 1, SIDE)
    z_far = lax.rem(z + 2, SIDE)
    neighbour = ((p, z_up), (p, z_down))
    z_source = (z_down, z_up)
    n_i, n_k, rows, n_b = amp.shape
    per_i = n_i // SIDE
    per_b = n_b // SIDE
    n_c = rows * PLANE
    depth = n_k * n_c
    pairs = n_i * n_k

    def place(offset):
        return lax.rem(x + offset[0] + SIDE, SIDE), lax.rem(y + offset[1] + SIDE, SIDE)

    def chip_at(offset):
        at_x, at_y = place(offset)
        return at_y * SIDE + at_x

    def back(offset):
        return (-offset[0], -offset[1])

    def via(dest, way):
        return (dest[0], 0) if way == 0 else (0, dest[1])

    def rest(dest, way):
        return (0, dest[1]) if way == 0 else (dest[0], 0)

    load_w = [pltpu.make_async_copy(wraw.at[k], wraw_v.at[k], load_sem.at[3 * k]) for k in range(n_k)]
    load_v = pltpu.make_async_copy(vint, v_v, load_sem.at[1])
    load_h = pltpu.make_async_copy(amp.at[:, :, pl.ds(0, 16), :], head_v, load_sem.at[2])
    for load in load_w:
        load.start()
    load_v.start()

    @pl.when(p == 0)
    def _():
        load_h.start()

    barrier = pltpu.get_barrier_semaphore()

    def greet(step, carry):
        pl.semaphore_signal(barrier, inc=1, device_id=(lax.rem(p + step, PLANE), z), device_id_type=MESH)
        return carry

    lax.fori_loop(1, PLANE, greet, 0)

    def greet_z(step, carry):
        pl.semaphore_signal(barrier, inc=1, device_id=(p, lax.rem(z + step, SIDE)), device_id_type=MESH)
        return carry

    lax.fori_loop(1, SIDE, greet_z, 0)

    r = lax.broadcasted_iota(jnp.int32, (256, 128), 0)
    c = lax.broadcasted_iota(jnp.int32, (256, 128), 1)
    pick = jnp.where(r == 2 * c + core, 1.0, 0.0).astype(BF16)
    groups = 128 // GROUP

    def owner_of(n):
        first, owner = n * GROUP % rows // GROUP, n * GROUP // rows
        return 2 * first + owner % 2, owner // 2

    def prep(lane, k):
        if lane == 0:
            load_w[k].wait()

        def turn(block, carry):
            at = pl.multiple_of(block * 128, 128)
            both = wraw_v[k, pl.ds(at, 128), :, lane * 128 : (lane + 1) * 128].reshape(256, 128)
            turned = lax.dot_general(both, pick, (((0,), (0,)), ((), ())), preferred_element_type=F32)
            turned = turned.astype(BF16)
            for n in range(groups):
                g, owner_x = owner_of(lane * groups + n)
                wt[z, g, owner_x, :, pl.ds(pl.multiple_of(k * n_c + at, 128), 128)] = turned[
                    n * GROUP : (n + 1) * GROUP
                ]
            return carry

        lax.fori_loop(0, n_c // 128, turn, 0, unroll=4)

    def w_copy(ref, g, way):
        return remote(ref, ref, wsend.at[way, g], wrecv.at[way, g], neighbour[way])

    def w_early(lane, k):
        for n in range(lane * groups, (lane + 1) * groups):
            g, owner_x = owner_of(n)
            if g < 2:
                for way in range(2):
                    w_copy(wt.at[z, g, owner_x, :, pl.ds(k * n_c, n_c)], g, way).start()

    prep(0, 0)
    pl.semaphore_wait(barrier, PLANE - 1 + SIDE - 1)
    w_early(0, 0)

    def a_rows(source_chip, source_core):
        return pl.ds(pl.multiple_of((2 * source_chip + source_core) * rows, rows), rows)

    def a_lanes(i):
        return pl.ds(i * per_b, per_b)

    def a_columns(at_x):
        return pl.ds(pl.multiple_of(at_x * per_b, per_b), per_b)

    def a_slot(n, way):
        return 2 * n + way

    def send_a_turned():
        for n, dest in enumerate(TURNED):
            at_x, at_y = place(dest)
            for way in WAYS:
                slot = a_slot(n, way)
                remote(
                    amp.at[pl.ds(at_y * per_i, per_i), way, :, a_columns(at_x)], a_relay.at[slot], s1.at[slot], rr.at[slot],
                    (2 * chip_at(via(dest, way)) + core, z),
                ).start()

    def send_a_straight():
        for n, dest in enumerate(STRAIGHT):
            at_x, at_y = place(dest)
            for i in range(per_i):
                remote(
                    amp.at[at_y * per_i + i, :, :, a_columns(at_x)], a_all.at[:, a_rows(chip, core), a_lanes(i)],
                    s2.at[n], r1.at[chip], (2 * chip_at(dest) + core, z),
                ).start()
        for i in range(per_i):
            pltpu.make_async_copy(
                amp.at[y * per_i + i, :, :, a_columns(x)], a_all.at[:, a_rows(chip, core), a_lanes(i)], r1.at[chip]
            ).start()

    def tile_down():
        for dy in range(1, SIDE):
            remote(tile_in, tile_in, tb_send.at[dy + 2], tb_recv, (2 * (dy * SIDE + x), z)).start()
        remote(tile_in, tile_in, tf_send, tb_recv, partner).start()

    @pl.when(p != 0)
    def _():
        send_a_turned()

    prep(0, 1)
    w_early(0, 1)

    @pl.when(p == 0)
    def _():
        load_h.wait()
        flat = head_v[...].reshape(pairs * 16, n_b)
        r = lax.broadcasted_iota(jnp.int32, (4 * pairs, pairs * 16), 0)
        c = lax.broadcasted_iota(jnp.int32, (4 * pairs, pairs * 16), 1)
        t = sum((r >= n * pairs).astype(jnp.int32) for n in range(1, 4))
        pick_row = jnp.where(c == 16 * (r - pairs * t) + t, 1.0, 0.0).astype(BF16)
        every = jnp.dot(pick_row, flat, preferred_element_type=F32).astype(BF16)
        for zz in range(SIDE):
            tile_out[zz] = every[:, zz * per_b : (zz + 1) * per_b]
        pltpu.make_async_copy(tile_out.at[z], tile_in.at[z], tz_recv.at[z]).start()

        def send_t(step, carry):
            zz = lax.rem(z + step, SIDE)
            remote(tile_out.at[zz], tile_in.at[z], tz_send.at[zz], tz_recv.at[z], (p, zz)).start()
            return carry

        lax.fori_loop(1, SIDE, send_t, 0)

    for k in range(n_k):
        prep(1, k)
        w_early(1, k)

    @pl.when(p == 0)
    def _():
        for zz in range(SIDE):
            await_bytes(tile_in.at[zz], tz_recv.at[zz])
        for dx in range(1, SIDE):
            remote(tile_in, tile_in, tb_send.at[dx - 1], tb_recv, (2 * dx, z)).start()
        tile_down()
        send_a_turned()

    for k in range(n_k):
        prep(2, k)
        w_early(2, k)

    @pl.when((y == 0) & (core == 0) & (x != 0))
    def _():
        await_bytes(tile_in, tb_recv)
        tile_down()

    send_a_straight()
    load_pair = pltpu.make_async_copy(pair_in, pair_v, pair_sem)
    load_pair.start()

    def w_start(g):
        for way in range(2):
            w_copy(wt.at[z, g], g, way).start()

    def w_half(source, g, way):
        return wt.at[source, g, pl.ds(2 * way, 2)]

    def w_pass(g):
        for way in range(2):
            await_bytes(wt.at[z_source[way], g], wrecv.at[way, g])
            ref = w_half(z_source[way], g, way)
            remote(ref, ref, wfsend.at[way, g], wfrecv.at[way, g], neighbour[way]).start()

    def w_far(g):
        for way in range(2):
            await_bytes(w_half(z_far, g, way), wfrecv.at[way, g])

    def pass_a(offsets):
        for offset in offsets:
            source = chip_at(back(offset))
            ref = a_all.at[:, a_rows(source, core), :]
            await_bytes(ref, r1.at[source])
            remote(ref, ref, sf.at[source], rf.at[source], partner).start()

    w_pass(0)
    w_start(2)

    for n, dest in enumerate(TURNED):
        for way in WAYS:
            slot = a_slot(n, way)
            await_bytes(a_relay.at[slot], rr.at[slot])
            source = chip_at(back(via(dest, way)))
            for i in range(per_i):
                remote(
                    a_relay.at[slot, i], a_all.at[way, a_rows(source, core), a_lanes(i)], rs.at[slot], r1.at[source],
                    (2 * chip_at(rest(dest, way)) + core, z),
                ).start()

    w_pass(1)
    w_start(3)

    @pl.when((y != 0) & (core == 0))
    def _():
        await_bytes(tile_in, tb_recv)
        remote(tile_in, tile_in, tf_send, tb_recv, partner).start()

    pass_a(((0, 0),) + STRAIGHT)

    row = lax.broadcasted_iota(jnp.int32, (rows, n_b), 0)
    col = lax.broadcasted_iota(jnp.int32, (rows, n_b), 1)
    mine = col == row + p * rows
    energy = jnp.broadcast_to(virt_e[...].reshape(1, n_b), (rows, n_b))
    table[0] = energy + jnp.sum(jnp.where(mine, energy, 0.0), axis=1, keepdims=True)
    blocks = virt_l.shape[1]
    first = lax.broadcasted_iota(jnp.int32, (blocks, n_b), 0) * VBLK
    at = lax.broadcasted_iota(jnp.int32, (blocks, n_b), 1)
    member = jnp.where((at >= first) & (at < first + VBLK), 1.0, 0.0).astype(BF16)
    labels = jnp.broadcast_to((virt_l[...] & 1).astype(F32).astype(BF16), (8, blocks))
    label = jnp.dot(labels, member, preferred_element_type=F32)
    label = jnp.broadcast_to(label[0:1], (rows, n_b))
    table[1] = jnp.abs(label - jnp.sum(jnp.where(mine, label, 0.0), axis=1, keepdims=True))

    w_pass(2)
    w_start(4)

    @pl.when(core == 1)
    def _():
        await_bytes(tile_in, tb_recv)

    load_v.wait()
    for zz in range(SIDE):
        total = None
        for t in range(4):
            right = v_v[:, t].reshape(4 * rows, per_b)
            term = lax.dot_general(
                tile_in[zz, t * pairs : (t + 1) * pairs], right, (((1,), (1,)), ((), ())), preferred_element_type=F32
            )
            total = term if total is None else total + term
        part[zz] = total
    pltpu.make_async_copy(part.at[z], part_in.at[z], p_recv.at[z]).start()

    def send_p(step, carry):
        zz = lax.rem(z + step, SIDE)
        remote(part.at[zz], part_in.at[z], p_send.at[zz], p_recv.at[z], (p, zz)).start()
        return carry

    lax.fori_loop(1, SIDE, send_p, 0)

    pass_a(TURNED)

    def got_a(source, carry):
        await_bytes(a_all.at[:, a_rows(source, 1 - core), :], rf.at[source])
        return carry

    lax.fori_loop(0, CHIPS, got_a, 0)

    def target(at_x, at_y, t, first=0, count=3):
        return coupled.at[
            pl.ds(at_y * per_i + first, count), core, pl.ds(t * GROUP, GROUP),
            pl.ds(pl.multiple_of(at_x * per_b, per_b), per_b),
        ]

    def share(g, way):
        first = 1 + g % 2
        return (0, first) if way == 0 else (first, per_i - first)

    def send_turned(g, way):
        first, count = share(g, way)
        for n, dest in enumerate(TURNED):
            remote(
                prod.at[g, chip_at(dest), pl.ds(first, count)], c_relay.at[g, n, pl.ds(first, count)],
                csend.at[g], crr.at[g, n, way], (2 * chip_at(via(dest, way)) + core, z),
            ).start()

    def send_straight(g):
        t = g // 2
        here = target(x, y, t)
        for dest in STRAIGHT:
            remote(prod.at[g, chip_at(dest)], here, csend.at[g], crecv.at[t], (2 * chip_at(dest) + g % 2, z)).start()
        if g % 2 == 1:
            remote(prod.at[2 * t + 1 - core, chip], here, cpsend.at[t], crecv.at[t], partner).start()
            pltpu.make_async_copy(prod.at[2 * t + core, chip], here, crecv.at[t]).start()

    def product(g):
        left = wt[:, g].reshape(CHIPS * GROUP, depth)

        def columns(start, size):
            right = a_all[:, :, start : start + size].reshape(depth, size)
            value = jnp.dot(left, right, preferred_element_type=F32).astype(BF16)
            for lane in range(0, size, 128):
                i, at = (start + lane) // per_b, (start + lane) % per_b
                prod[g, :, i, :, at : at + 128] = value[:, lane : lane + 128].reshape(CHIPS, GROUP, 128)

        if g == PARTS - 1:
            cut = (1 + g % 2) * per_b
            columns(0, cut)
            send_turned(g, 0)
            columns(cut, per_i * per_b - cut)
            send_turned(g, 1)
        else:
            columns(0, per_i * per_b)
            send_turned(g, 0)
            send_turned(g, 1)
        send_straight(g)

    def pass_c(g):
        for n, dest in enumerate(TURNED):
            for way in WAYS:
                first, count = share(g, way)
                ref = c_relay.at[g, n, pl.ds(first, count)]
                await_bytes(ref, crr.at[g, n, way])
                at_x, at_y = place(back(via(dest, way)))
                owner = 2 * chip_at(rest(dest, way)) + g % 2
                remote(ref, target(at_x, at_y, g // 2, first, count), crs.at[g], crecv.at[g // 2], (owner, z)).start()

    def group_rows(t):
        return pl.ds(t * GROUP, GROUP)

    def update_rows(t):
        await_bytes(coupled.at[:, :, group_rows(t), :], crecv.at[t])
        block = slice(t * GROUP, (t + 1) * GROUP)

        def update(with_ladder):
            def step(i, carry):
                energy_i = occ_e[slab_i[i]]
                label_i = occ_l[slab_i[i]]
                for j in range(n_k):
                    energy = energy_i + occ_e[slab_j[j]]
                    odd = ((label_i + occ_l[slab_j[j]]) & 1).astype(F32)
                    value = coupled[i, j, block].astype(F32)
                    if with_ladder:
                        term = jnp.concatenate(
                            [lad_v[a, pl.ds(i * n_k + j, 1), :] for a in range(4)]
                            + [jnp.zeros((GROUP - 4, n_b), F32)],
                            axis=0,
                        )
                        value = (value + term).astype(BF16).astype(F32)
                    residual = pair_v[i, j, block].astype(F32) + value
                    allowed = (1.0 - odd) + (2.0 * odd - 1.0) * table[1, block]
                    out_v[i, j, block] = (allowed * residual / (table[0, block] - energy)).astype(BF16)
                pltpu.make_async_copy(
                    out_v.at[i, :, group_rows(t), :], out.at[i, :, group_rows(t), :], out_sem.at[t]
                ).start()
                return carry

            lax.fori_loop(0, n_i, step, 0)

        if t == 0:

            @pl.when(p == 0)
            def _():
                update(True)

            @pl.when(p != 0)
            def _():
                update(False)

        else:
            update(False)

    w_far(0)
    product(0)
    w_far(1)
    product(1)
    w_pass(3)
    w_start(5)
    pass_c(0)
    pass_c(1)

    w_far(2)
    product(2)
    w_pass(4)
    pass_c(2)

    for zz in range(SIDE):
        await_bytes(part_in.at[zz], p_recv.at[zz])
    sum_v[...] = part_in[0] + part_in[1] + part_in[2] + part_in[3]

    @pl.when(p == 0)
    def _():
        pltpu.make_async_copy(sum_v, fin_in.at[0], f_recv).start()

    @pl.when(p != 0)
    def _():
        remote(sum_v, fin_in.at[p], f_send, f_recv, (0, z)).start()

    w_far(3)
    product(3)

    w_pass(5)
    pass_c(3)

    @pl.when(p == 0)
    def _():
        await_bytes(fin_in, f_recv)
        for q in range(PLANE):
            for a in range(4):
                lad_v[a, :, q * rows : (q + 1) * rows] = fin_in[q, :, a * rows : (a + 1) * rows]


    load_pair.wait()
    update_rows(0)
    w_far(4)
    product(4)
    w_far(5)
    product(5)
    pass_c(4)
    pass_c(5)
    update_rows(1)
    update_rows(2)

    for slot in range(2 * len(TURNED)):
        await_bytes(a_relay.at[slot], s1.at[slot])
        await_bytes(a_relay.at[slot], rs.at[slot])
    for n in range(len(STRAIGHT)):
        await_bytes(a_all.at[:, pl.ds(0, rows), :], s2.at[n])

    def passed_a(step, carry):
        await_bytes(a_all.at[:, a_rows(step, core), :], sf.at[step])
        return carry

    lax.fori_loop(0, CHIPS, passed_a, 0)
    for way in range(2):
        for g in range(PARTS):
            await_bytes(wt.at[z, g], wsend.at[way, g])
            await_bytes(w_half(z, g, way), wfsend.at[way, g])

    def sent_p(step, carry):
        zz = lax.rem(z + step, SIDE)
        await_bytes(part.at[zz], p_send.at[zz])
        return carry

    lax.fori_loop(1, SIDE, sent_p, 0)

    @pl.when(core == 0)
    def _():
        await_bytes(tile_in, tf_send)

    @pl.when((y == 0) & (core == 0))
    def _():
        for dy in range(1, SIDE):
            await_bytes(tile_in, tb_send.at[dy + 2])

    @pl.when(p == 0)
    def _():
        def sent_t(step, carry):
            zz = lax.rem(z + step, SIDE)
            await_bytes(tile_out.at[zz], tz_send.at[zz])
            return carry

        lax.fori_loop(1, SIDE, sent_t, 0)
        for dx in range(1, SIDE):
            await_bytes(tile_in, tb_send.at[dx - 1])

    @pl.when(p != 0)
    def _():
        await_bytes(sum_v, f_send)

    for g in range(PARTS):
        await_bytes(prod.at[g, pl.ds(0, CHIPS - 1)], csend.at[g])
        await_bytes(c_relay.at[g], crs.at[g])
    for t in range(PARTS // 2):
        await_bytes(prod.at[t, 0], cpsend.at[t])
    for t in range(PARTS // 2):
        await_bytes(out_v.at[:, :, group_rows(t), :], out_sem.at[t])


def exchange(amp, wraw, vint, pair, virt_e, virt_l, occ_e, occ_l, slab_i, slab_j):
    n_i, n_k, rows, n_b = amp.shape
    per_i, per_b, n_c = n_i // SIDE, n_b // SIDE, rows * PLANE
    pairs, turned = n_i * n_k, len(TURNED)
    dma = pltpu.SemaphoreType.DMA
    anywhere = pl.BlockSpec(memory_space=pl.ANY)
    inside = pl.BlockSpec(memory_space=pltpu.VMEM)
    return pl.pallas_call(
        exchange_kernel,
        out_shape=jax.ShapeDtypeStruct(amp.shape, BF16),
        in_specs=[anywhere] * 4 + [inside] * 2 + [pl.BlockSpec(memory_space=pltpu.SMEM)] * 4,
        out_specs=anywhere,
        scratch_shapes=[
            pltpu.VMEM(amp.shape, BF16),
            pltpu.VMEM(amp.shape, BF16),
            pltpu.VMEM(amp.shape, BF16),
            pltpu.VMEM(wraw.shape, BF16),
            pltpu.VMEM(vint.shape, BF16),
            pltpu.VMEM((n_i, n_k, 16, n_b), BF16),
            pltpu.VMEM((SIDE, PARTS, SIDE, GROUP, n_k * n_c), BF16),
            pltpu.VMEM((n_k, n_c, per_i * per_b), BF16),
            pltpu.VMEM((PARTS, CHIPS, per_i, GROUP, per_b), BF16),
            pltpu.VMEM((2 * turned, per_i, rows, per_b), BF16),
            pltpu.VMEM((PARTS, turned, per_i, GROUP, per_b), BF16),
            pltpu.VMEM((SIDE, 4 * pairs, per_b), BF16),
            pltpu.VMEM((SIDE, 4 * pairs, per_b), BF16),
            pltpu.VMEM((SIDE, pairs, 4 * rows), F32),
            pltpu.VMEM((SIDE, pairs, 4 * rows), F32),
            pltpu.VMEM((pairs, 4 * rows), F32),
            pltpu.VMEM((PLANE, pairs, 4 * rows), F32),
            pltpu.VMEM((4, pairs, n_b), F32),
            pltpu.VMEM((2, rows, n_b), F32),
            dma((4,)),
            dma((2 * turned,)),
            dma((len(STRAIGHT),)),
            dma((CHIPS,)),
            dma((2 * turned,)),
            dma((2 * turned,)),
            dma((CHIPS,)),
            dma((CHIPS,)),
            dma((2, PARTS)),
            dma((2, PARTS)),
            dma((2, PARTS)),
            dma((2, PARTS)),
            dma((PARTS,)),
            dma((PARTS // 2,)),
            dma((PARTS // 2,)),
            dma((PARTS,)),
            dma((PARTS, turned, 2)),
            dma,
            dma((PARTS // 2,)),
            dma((SIDE,)),
            dma((SIDE,)),
            dma((6,)),
            dma,
            dma,
            dma((SIDE,)),
            dma((SIDE,)),
            dma,
            dma,
        ],
        compiler_params=pltpu.CompilerParams(
            collective_id=0, has_side_effects=True, vmem_limit_bytes=60 * 1024 * 1024
        ),
        name="exchange",
    )(amp, wraw, vint, pair, virt_e, virt_l.reshape(1, -1), occ_e, occ_l, slab_i, slab_j)


def per_device(
    amplitudes,
    pair_integrals,
    cycle_integrals,
    ladder_integrals,
    occ_energy,
    virt_energy,
    occ_irrep,
    virt_irrep,
    slab_i,
    slab_j,
):
    return exchange(
        amplitudes, cycle_integrals, ladder_integrals, pair_integrals, virt_energy, virt_irrep, occ_energy, occ_irrep,
        slab_i, slab_j,
    )


def solution(mesh):
    return jax.shard_map(
        per_device,
        mesh=mesh,
        in_specs=(
            P("narrow", None, "wide", None),
            P("narrow", None, "wide", None),
            P(None, None, None, "narrow"),
            P(None, None, "wide", "narrow"),
            P(),
            P(),
            P(),
            P(),
            P("narrow"),
            P(),
        ),
        out_specs=P("narrow", None, "wide", None),
        check_vma=False,
    )
```
